128 devices in a mesh: row: 8 (over x_lo, y), col: 16 (over x_hi, z, core).
Axes of the slice: x: 4 (x_hi: 2, x_lo: 2; x = x_hi * 2 + x_lo), y: 4, z: 4, core: 2. Of those that a mesh axis runs over, the one named last changes fastest.
Arguments:
- query_acts: bfloat16 [2048, 6144], P('col', 'row'), may hold values from -6 to 6
- query_grads: bfloat16 [2048, 6144], P('row', 'col'), may hold values from -6 to 6
- act_basis: bfloat16 [6144, 6144], P('row', 'col'), may hold values from -0.078125 to 0.078125
- grad_basis: bfloat16 [6144, 6144], P('col', 'row'), may hold values from -0.078125 to 0.078125
- eigenvalues: float32 [6144, 6144], P('row', 'col'), may hold values from 0.05 to 5
- train_acts: bfloat16 [2560, 6144], P('row', 'col'), may hold values from -6 to 6
- train_grads: bfloat16 [2560, 6144], P('col', 'row'), may hold values from -6 to 6
Outputs:
- scores: float32 [8, 2560], P(None, ('row', 'col'))
The draws below stay inside these ranges and needn't reach their ends.
All inputs are finite; a program needn't handle non-finite values.
Results may differ from the reference program's by a relative error of at most 0.012.
Values may be sent and summed in bfloat16 or wider, within the bound.
A program may use at most 64 MiB of HBM per device.

```python
import math
import jax
import jax.numpy as jnp
from jax import lax

D = 6144
QUERIES = 8
QUERY_LEN = 256
QUERY_TOKENS = 2048
TRAIN_TOKENS = 2560


def scaled_rows(key, salt, rows, cols):
    inner = jax.random.fold_in(key, salt)
    first = jax.random.fold_in(inner, 0)
    values = jax.random.truncated_normal(first, -4.0, 4.0, (rows, cols), jnp.float32)
    return values.astype(jnp.bfloat16)


def draw_query_acts(key, part):
    return scaled_rows(key, 101, QUERY_TOKENS, D)


def draw_query_grads(key, part):
    return scaled_rows(key, 202, QUERY_TOKENS, D)


def draw_train_acts(key, part):
    return scaled_rows(key, 303, TRAIN_TOKENS, D)


def draw_train_grads(key, part):
    return scaled_rows(key, 404, TRAIN_TOKENS, D)


def level_of(own_key, shape, cuts, least, top_value):
    def one(dim, shards_of):
        steps = jax.random.uniform(jax.random.fold_in(jax.random.fold_in(own_key, 6), dim), (shards_of,), jnp.float32, least / len(cuts), top_value / len(cuts))
        return jnp.repeat(jnp.exp(steps), shape[dim] // shards_of).reshape((-1,) + (1,) * (len(shape) - dim - 1))

    factor_of = one(*cuts[0])
    for cut in cuts[1:]:
        factor_of = factor_of * one(*cut)
    return factor_of


def noise(rng, dims, scale, reach, pieces=(), kind=jnp.bfloat16):
    entries = jax.random.normal(rng, dims, jnp.float32) * scale
    if len(pieces) > 0:
        entries = level_of(rng, dims, pieces, -0.22, 0.18) * entries
    return jnp.clip(entries, min=-reach, max=reach).astype(kind)


def setup_inputs(seed: int = 0) -> dict:
    splits = jax.random.split(jax.random.key(seed), 8)
    query_acts = draw_query_acts(jax.random.fold_in(splits[7], 71), 0)
    query_grads = draw_query_grads(jax.random.fold_in(splits[7], 71), 0)
    act_basis = noise(splits[2], (D, D), D ** -0.5, 0.078125, ((0, 8), (1, 16)))
    grad_basis = noise(splits[3], (D, D), D ** -0.5, 0.078125, ((0, 16), (1, 8)))
    eigenvalues = jnp.clip(jnp.exp(math.log(5.0) - 4.6051702 * jax.random.uniform(splits[4], (D, D), jnp.float32) ** level_of(splits[4], (D, D), ((0, 8), (1, 16)), -0.2, 0.2)), 0.05, 5.0)
    train_acts = draw_train_acts(jax.random.fold_in(splits[7], 71), 0)
    train_grads = draw_train_grads(jax.random.fold_in(splits[7], 71), 0)
    return dict(query_acts=query_acts, query_grads=query_grads, act_basis=act_basis, grad_basis=grad_basis, eigenvalues=eigenvalues, train_acts=train_acts, train_grads=train_grads)


damping = 0.01


def reference(query_acts, query_grads, act_basis, grad_basis, eigenvalues, train_acts, train_grads):
    rot_acts = jnp.dot(query_acts, act_basis, preferred_element_type=jnp.float32).astype(jnp.bfloat16)
    rot_grads = jnp.dot(query_grads, grad_basis, preferred_element_type=jnp.float32).astype(jnp.bfloat16)

    def one_query(index):
        start = (index * QUERY_LEN).astype(jnp.int32)
        grads_q = lax.dynamic_slice_in_dim(rot_grads, start, QUERY_LEN, 0)
        acts_q = lax.dynamic_slice_in_dim(rot_acts, start, QUERY_LEN, 0)
        outer = jnp.dot(grads_q.T, acts_q, preferred_element_type=jnp.float32)
        panel = (outer / (QUERY_LEN * (eigenvalues + damping))).astype(jnp.bfloat16)
        mapped = jnp.dot(train_acts, panel.T, preferred_element_type=jnp.float32)
        return jnp.sum(mapped * train_grads.astype(jnp.float32), axis=1) / D

    return lax.map(one_query, jnp.arange(QUERIES, dtype=jnp.int32))
```

```python
import jax
import jax.numpy as jnp
from jax import lax
from jax.experimental import pallas as pl
from jax.experimental.pallas import tpu as pltpu
from jax.sharding import PartitionSpec as P

D = 6144
QUERY_LEN = 256
QUERIES = 8
DAMPING = 0.01

ROWS = 8
COLS = 16
TILE_I = D // ROWS
TILE_J = D // COLS
TOKENS = QUERIES * QUERY_LEN
TRAIN = 2560
BLOCK = TRAIN // 8
OWNED = TRAIN // (ROWS * COLS)

CHUNKS = 4
PER_CHUNK = QUERIES // CHUNKS
CHUNK_TOKENS = PER_CHUNK * QUERY_LEN
PIECE = CHUNK_TOKENS // 4
HALF = PIECE // 2

MESH = pl.DeviceIdType.MESH
BF16 = jnp.bfloat16
F32 = jnp.float32

AG_A, AG_G, AG_TA, AG_TG = 0, 9, 18, 27
SIB_A, SIB_G, SIB_TG = 36, 44, 52
SIB_BASIS = 60
REDUCE = 61
PER_REDUCE = 10
FIRST = REDUCE + 2 * CHUNKS * PER_REDUCE
SECOND = FIRST + ROWS - 1
N_SEMS = SECOND + COLS - 1


def kernel(
    qa_ref, qg_ref, ab_ref, gb_ref, eig_ref, ta_ref, tg_ref, out_ref,
    qa, qg, ab, gb, rcp, ta, tg, part, rot_a, rot_g, near, mid, mine, other,
    panels, acc, first, split, second, local, sent, got,
):
    r = lax.axis_index("row")
    c = lax.axis_index("col")
    xl, y = r // 4, r % 4
    xh, z, k = c // 8, (c // 2) % 4, c % 2
    sib = (r, c + 1 - 2 * k)

    class Group:
        pass

    row_g, col_g = Group(), Group()
    row_g.p, row_g.u = xl, y
    row_g.up, row_g.dn = (xl * 4 + (y + 1) % 4, c), (xl * 4 + (y + 3) % 4, c)
    row_g.pair = ((1 - xl) * 4 + y, c)
    col_g.p, col_g.u = xh, z
    col_g.up = (r, xh * 8 + ((z + 1) % 4) * 2 + k)
    col_g.dn = (r, xh * 8 + ((z + 3) % 4) * 2 + k)
    col_g.pair = (r, (1 - xh) * 8 + z * 2 + k)

    def remote(src, dst, i, dev):
        return pltpu.make_async_remote_copy(
            src_ref=src, dst_ref=dst, send_sem=sent.at[i], recv_sem=got.at[i],
            device_id=dev, device_id_type=MESH,
        )

    def lanes(core):
        return pl.ds(pl.multiple_of(core * TILE_J, TILE_J), TILE_J)

    def rows_of(ref, core, size):
        def view(slot, lo, n):
            return ref.at[slot, pl.ds(pl.multiple_of(core * size + lo, 16), n)]

        return view

    def lanes_of(ref, core):
        def view(slot, lo, n):
            return ref.at[slot, pl.ds(lo, n), lanes(core)]

        return view

    def whole(ref):
        def view(slot, lo, n):
            return ref.at[slot, pl.ds(lo, n)]

        return view

    class Gather:
        def __init__(self, g, src, view, view_sib, n, base, sib_base):
            self.g, self.src, self.view, self.view_sib = g, src, view, view_sib
            self.n, self.base, self.sib_base = n, base, sib_base
            p, u = g.p, g.u
            self.own, self.q1 = p * 4 + u, (1 - p) * 4 + u
            m, o, w = (u + 3) % 4, (u + 1) % 4, (u + 2) % 4
            self.low = (p * 4 + m, (1 - p) * 4 + m)
            self.high = (p * 4 + o, (1 - p) * 4 + o)
            self.far = (p * 4 + w, (1 - p) * 4 + w)

        def full(self, slot):
            return self.view(slot, 0, self.n)

        def half(self, slot, h):
            return self.view(slot, h * (self.n // 2), self.n // 2)

        def copies(self, stage):
            g, b = self.g, self.base
            if stage == "pair":
                return [(self.src, self.full(self.own), b, g.pair)]
            if stage == "near0":
                return [
                    (self.src, self.full(self.own), b + 1, g.up),
                    (self.src, self.full(self.own), b + 2, g.dn),
                ]
            if stage == "near1":
                v = self.full(self.q1)
                return [(v, v, b + 3, g.up), (v, v, b + 4, g.dn)]
            i = 0 if stage == "far0" else 1
            lo, hi = self.half(self.low[i], 0), self.half(self.high[i], 1)
            return [(lo, lo, b + 5 + 2 * i, g.up), (hi, hi, b + 6 + 2 * i, g.dn)]

        def start(self, stage):
            for a in self.copies(stage):
                remote(*a).start()

        def wait_send(self):
            for stage in ("pair", "near0", "near1", "far0", "far1"):
                for a in self.copies(stage):
                    remote(*a).wait_send()

        def wait(self, stage):
            b, g = self.base, self.g
            if stage == "pair":
                got_ = [(self.full(self.q1), b, g.pair)]
            elif stage in ("near0", "near1"):
                i = 0 if stage == "near0" else 1
                got_ = [
                    (self.full(self.low[i]), b + 1 + 2 * i, g.dn),
                    (self.full(self.high[i]), b + 2 + 2 * i, g.up),
                ]
            else:
                i = 0 if stage == "far0" else 1
                got_ = [
                    (self.half(self.far[i], 0), b + 5 + 2 * i, g.dn),
                    (self.half(self.far[i], 1), b + 6 + 2 * i, g.up),
                ]
            for v, i, dev in got_:
                remote(v, v, i, dev).wait_recv()

        def slots(self):
            return (
                self.own, self.q1, self.low[0], self.high[0],
                self.low[1], self.high[1], self.far[0], self.far[1],
            )

        def sib_copy(self, j):
            slot = self.slots()[j]
            src = self.src if j == 0 else self.full(slot)
            return remote(src, self.full(slot), self.sib_base + j, sib)

        def sib_start(self, *js):
            for j in js:
                self.sib_copy(j).start()

        def sib_wait(self):
            for j, slot in enumerate(self.slots()):
                v = self.view_sib(slot, 0, self.n)
                remote(v, v, self.sib_base + j, sib).wait_recv()

        def sib_wait_send(self):
            for j in range(8):
                self.sib_copy(j).wait_send()

    half_q, half_t = QUERY_LEN // 2, BLOCK // 2
    g_qa = Gather(col_g, qa_ref, rows_of(qa, k, half_q), rows_of(qa, 1 - k, half_q), half_q, AG_A, SIB_A)
    g_qg = Gather(row_g, qg_ref, lanes_of(qg, k), lanes_of(qg, 1 - k), QUERY_LEN, AG_G, SIB_G)
    g_ta = Gather(row_g, ta_ref, whole(ta), None, BLOCK, AG_TA, None)
    g_tg = Gather(col_g, tg_ref, rows_of(tg, k, half_t), rows_of(tg, 1 - k, half_t), half_t, AG_TG, SIB_TG)
    queries, trains = (g_qa, g_qg), (g_ta, g_tg)

    copies = [
        pltpu.make_async_copy(eig_ref, rcp, local.at[0]),
        pltpu.make_async_copy(qa_ref, g_qa.full(g_qa.own), local.at[1]),
        pltpu.make_async_copy(qg_ref, g_qg.full(g_qg.own), local.at[2]),
        pltpu.make_async_copy(ab_ref, ab, local.at[3]),
        pltpu.make_async_copy(
            gb_ref.at[:, lanes(k)], gb.at[pl.ds(pl.multiple_of(k * TILE_J, TILE_J), TILE_J)], local.at[4]
        ),
        pltpu.make_async_copy(ta_ref, g_ta.full(g_ta.own), local.at[5]),
        pltpu.make_async_copy(tg_ref, g_tg.full(g_tg.own), local.at[6]),
    ]

    barrier = pltpu.get_barrier_semaphore()
    row_peers = [((r + d) % ROWS, c) for d in range(1, ROWS)]
    col_peers = [(r, (c + d) % COLS) for d in range(1, COLS)]
    for dev in row_peers + col_peers:
        pl.semaphore_signal(barrier, inc=1, device_id=dev, device_id_type=MESH)
    for cp in copies:
        cp.start()
    pl.semaphore_wait(barrier, ROWS + COLS - 2)

    for g in queries:
        g.start("pair")
    for g in queries:
        g.start("near0")
        g.sib_start(0)
    own_basis = gb.at[pl.ds(pl.multiple_of(k * TILE_J, TILE_J), TILE_J)]
    sib_basis = gb.at[pl.ds(pl.multiple_of((1 - k) * TILE_J, TILE_J), TILE_J)]
    basis_copy = remote(gb_ref.at[:, lanes(1 - k)], own_basis, SIB_BASIS, sib)
    basis_copy.start()
    for g in trains:
        g.start("near0")
    g_tg.sib_start(0)

    copies[0].wait()
    rcp[...] = 1.0 / (QUERY_LEN * (rcp[...] + DAMPING))

    for g in queries:
        g.wait("near0")
        g.start("far0")
        g.sib_start(2, 3)
    for g in queries:
        g.wait("pair")
        g.start("near1")
        g.sib_start(1)
    for g in trains:
        g.start("pair")
    for g in trains:
        g.wait("near0")
        g.start("far0")
    g_tg.sib_start(2, 3)
    for g in queries:
        g.wait("near1")
        g.start("far1")
        g.sib_start(4, 5)
    for g in queries:
        g.wait("far0")
        g.wait("far1")
        g.sib_start(6, 7)
    for g in queries:
        g.sib_wait()
    remote(sib_basis, sib_basis, SIB_BASIS, sib).wait_recv()
    for cp in copies[1:]:
        cp.wait()

    kinds = ((0, row_g), (1, col_g))

    def sem(t, ch, j):
        return REDUCE + (ch * 2 + t) * PER_REDUCE + j

    def rows(ch, v, lo=0, n=PIECE):
        return pl.ds(pl.multiple_of(ch * CHUNK_TOKENS + v * PIECE + lo, 16), n)

    def rotated(t, ds):
        if t == 0:
            return rot_a.at[ds]
        return rot_g.at[ds, lanes(k)]

    def at(g, d):
        return (g.u + d) % 4

    def reduce_copies(t, g, ch, step):
        if step == 1:
            v = at(g, 2)
            return [
                (part.at[t, rows(ch, v, 0, HALF)], near.at[t, ch, 0], sem(t, ch, 0), g.up),
                (part.at[t, rows(ch, v, HALF, HALF)], near.at[t, ch, 1], sem(t, ch, 1), g.dn),
            ]
        if step == 2:
            return [
                (part.at[t, rows(ch, at(g, 1))], mid.at[t, ch, 0], sem(t, ch, 2), g.up),
                (part.at[t, rows(ch, at(g, 3))], mid.at[t, ch, 1], sem(t, ch, 3), g.dn),
            ]
        if step == 3:
            return [(mine.at[t, ch], other.at[t, ch], sem(t, ch, 4), g.pair)]
        if step == 4:
            v = rotated(t, rows(ch, g.u))
            return [(v, v, sem(t, ch, 5), g.up), (v, v, sem(t, ch, 6), g.dn)]
        lo = rotated(t, rows(ch, at(g, 3), 0, HALF))
        hi = rotated(t, rows(ch, at(g, 1), HALF, HALF))
        return [(lo, lo, sem(t, ch, 7), g.up), (hi, hi, sem(t, ch, 8), g.dn)]

    def reduce_start(t, g, ch, step):
        for a in reduce_copies(t, g, ch, step):
            remote(*a).start()

    def landed(v, i, dev):
        remote(v, v, i, dev).wait_recv()

    def chunk_rows(ch):
        return pl.ds(pl.multiple_of(ch * CHUNK_TOKENS, 16), CHUNK_TOKENS)

    def sib_rot(ch):
        v = rot_g.at[chunk_rows(ch), lanes(k)]
        return remote(v, v, sem(1, ch, 9), sib)

    def partials(ch, carry):
        for i in range(PER_CHUNK):
            q = ch * PER_CHUNK + i
            ds = pl.ds(pl.multiple_of(q * QUERY_LEN, QUERY_LEN), QUERY_LEN)
            part[0, ds] = jnp.dot(qa[q], ab[...], preferred_element_type=F32).astype(BF16)
            part[1, ds] = jnp.dot(qg[q], gb[...], preferred_element_type=F32).astype(BF16)
        for t, g in kinds:
            reduce_start(t, g, ch, 1)
        return carry

    lax.fori_loop(0, CHUNKS, partials, 0)

    for g in trains:
        g.wait("pair")
        g.start("near1")
    g_tg.sib_start(1)

    def step2(ch):
        for t, g in kinds:
            landed(near.at[t, ch, 0], sem(t, ch, 0), g.dn)
            ds = rows(ch, at(g, 1), 0, HALF)
            part[t, ds] = (part[t, ds].astype(F32) + near[t, ch, 0].astype(F32)).astype(BF16)
            landed(near.at[t, ch, 1], sem(t, ch, 1), g.up)
            ds = rows(ch, at(g, 3), HALF, HALF)
            part[t, ds] = (part[t, ds].astype(F32) + near[t, ch, 1].astype(F32)).astype(BF16)
            reduce_start(t, g, ch, 2)

    def step3(ch):
        for t, g in kinds:
            landed(mid.at[t, ch, 0], sem(t, ch, 2), g.dn)
            landed(mid.at[t, ch, 1], sem(t, ch, 3), g.up)
            total = part[t, rows(ch, g.u)].astype(F32) + mid[t, ch, 0].astype(F32) + mid[t, ch, 1].astype(F32)
            mine[t, ch] = total.astype(BF16)
            reduce_start(t, g, ch, 3)

    def step4(ch):
        for t, g in kinds:
            landed(other.at[t, ch], sem(t, ch, 4), g.pair)
            total = (mine[t, ch].astype(F32) + other[t, ch].astype(F32)).astype(BF16)
            if t == 0:
                rot_a[rows(ch, g.u)] = total
            else:
                rot_g[rows(ch, g.u), lanes(k)] = total
            reduce_start(t, g, ch, 4)

    def step5(ch):
        for t, g in kinds:
            landed(rotated(t, rows(ch, at(g, 3))), sem(t, ch, 5), g.dn)
            landed(rotated(t, rows(ch, at(g, 1))), sem(t, ch, 6), g.up)
            reduce_start(t, g, ch, 5)

    def step6(ch):
        for t, g in reversed(kinds):
            landed(rotated(t, rows(ch, at(g, 2), 0, HALF)), sem(t, ch, 7), g.dn)
            landed(rotated(t, rows(ch, at(g, 2), HALF, HALF)), sem(t, ch, 8), g.up)
            if t == 1:
                sib_rot(ch).start()

    def make_panels(ch):
        v = rot_g.at[chunk_rows(ch), lanes(1 - k)]
        landed(v, sem(1, ch, 9), sib)
        for i in range(PER_CHUNK):
            ds = pl.ds(pl.multiple_of((ch * PER_CHUNK + i) * QUERY_LEN, QUERY_LEN), QUERY_LEN)
            outer = lax.dot_general(
                rot_g[ds], rot_a[ds], (((0,), (0,)), ((), ())), preferred_element_type=F32
            )
            panels[:, pl.ds(i * TILE_J, TILE_J)] = (outer * rcp[...]).astype(BF16)

    def score(ch, lo, hi):
        q_of = lax.broadcasted_iota(jnp.int32, (QUERIES, PER_CHUNK * 128), 0)
        lane = lax.broadcasted_iota(jnp.int32, (QUERIES, PER_CHUNK * 128), 1)
        pick = jnp.where(q_of == ch * PER_CHUNK + lane // 128, 1.0, 0.0).astype(BF16)

        def tile(tt, carry):
            mapped = jnp.dot(tg[tt], panels[...], preferred_element_type=F32)
            acts = ta[tt].astype(F32)
            sums = []
            for i in range(PER_CHUNK):
                total = None
                for j in range(TILE_J // 128):
                    term = mapped[:, i * TILE_J + j * 128 : i * TILE_J + (j + 1) * 128] * acts[:, j * 128 : (j + 1) * 128]
                    total = term if total is None else total + term
                sums.append(total.astype(BF16))
            lanes_sum = sums[0] if PER_CHUNK == 1 else jnp.concatenate(sums, axis=1)
            acc[tt] += lax.dot_general(
                pick, lanes_sum, (((1,), (1,)), ((), ())), preferred_element_type=F32
            )
            return carry

        lax.fori_loop(lo, hi, tile, 0)

    acc[...] = jnp.zeros_like(acc)

    def group(i, carry):
        def when(ch, f):
            @pl.when((ch >= 0) & (ch < CHUNKS))
            def _():
                f(ch)

        when(i - 1, step5)
        when(i, step2)
        when(i - 2, lambda ch: score(ch, 0, 4))
        when(i - 1, step6)
        when(i, step3)
        when(i - 2, lambda ch: score(ch, 4, 8))
        when(i, step4)

        @pl.when(i == 0)
        def _():
            for g in trains:
                g.wait("near1")
                g.start("far1")
            g_tg.sib_start(4, 5)

        @pl.when(i == 1)
        def _():
            for g in trains:
                g.wait("far0")
                g.wait("far1")
            g_tg.sib_start(6, 7)
            g_tg.sib_wait()

        when(i - 1, make_panels)
        return carry

    lax.fori_loop(0, CHUNKS + 2, group, 0)

    def to_row(d):
        peer = (r + d) % ROWS
        return remote(acc.at[peer], first.at[d - 1], FIRST + d - 1, (peer, c))

    for d in range(1, ROWS):
        to_row(d).start()
    total = acc[r]
    for d in range(1, ROWS):
        landed(first.at[d - 1], FIRST + d - 1, ((r + ROWS - d) % ROWS, c))
        total = total + first[d - 1]
    total = total / D
    for j in range(COLS):
        split[j] = total[:, j * OWNED : (j + 1) * OWNED]

    def to_col(d):
        peer = (c + d) % COLS
        return remote(split.at[peer], second.at[d - 1], SECOND + d - 1, (r, peer))

    for d in range(1, COLS):
        to_col(d).start()
    total = split[c]
    for d in range(1, COLS):
        landed(second.at[d - 1], SECOND + d - 1, (r, (c + COLS - d) % COLS))
        total = total + second[d - 1]
    out_ref[...] = total

    for g in queries + trains:
        g.wait_send()
    for g in (g_qa, g_qg, g_tg):
        g.sib_wait_send()
    basis_copy.wait_send()

    def drain(ch, carry):
        for t, g in kinds:
            for step in range(1, 6):
                for a in reduce_copies(t, g, ch, step):
                    remote(*a).wait_send()
        sib_rot(ch).wait_send()
        return carry

    lax.fori_loop(0, CHUNKS, drain, 0)
    for d in range(1, ROWS):
        to_row(d).wait_send()
    for d in range(1, COLS):
        to_col(d).wait_send()


def shards(*args):
    any_spec = pl.BlockSpec(memory_space=pl.ANY)
    vmem = pltpu.VMEM
    return pl.pallas_call(
        kernel,
        out_shape=jax.ShapeDtypeStruct((QUERIES, OWNED), F32),
        in_specs=[any_spec] * 7,
        out_specs=pl.BlockSpec(memory_space=pltpu.VMEM),
        scratch_shapes=[
            vmem((8, QUERY_LEN, TILE_I), BF16),
            vmem((8, QUERY_LEN, 2 * TILE_J), BF16),
            vmem((TILE_I, TILE_J), BF16),
            vmem((2 * TILE_J, TILE_J), BF16),
            vmem((TILE_I, TILE_J), F32),
            vmem((8, BLOCK, TILE_J), BF16),
            vmem((8, BLOCK, TILE_I), BF16),
            vmem((2, TOKENS, TILE_J), BF16),
            vmem((TOKENS, TILE_J), BF16),
            vmem((TOKENS, TILE_I), BF16),
            vmem((2, CHUNKS, 2, HALF, TILE_J), BF16),
            vmem((2, CHUNKS, 2, PIECE, TILE_J), BF16),
            vmem((2, CHUNKS, PIECE, TILE_J), BF16),
            vmem((2, CHUNKS, PIECE, TILE_J), BF16),
            vmem((TILE_I, PER_CHUNK * TILE_J), BF16),
            vmem((8, QUERIES, BLOCK), F32),
            vmem((ROWS - 1, QUERIES, BLOCK), F32),
            vmem((COLS, QUERIES, OWNED), F32),
            vmem((COLS - 1, QUERIES, OWNED), F32),
            pltpu.SemaphoreType.DMA((7,)),
            pltpu.SemaphoreType.DMA((N_SEMS,)),
            pltpu.SemaphoreType.DMA((N_SEMS,)),
        ],
        compiler_params=pltpu.CompilerParams(
            collective_id=0, has_side_effects=True, vmem_limit_bytes=50 * 1024 * 1024
        ),
        name="influence",
    )(*args)


def solution(mesh):
    return jax.shard_map(
        shards,
        mesh=mesh,
        in_specs=(
            P("col", "row"),
            P("row", "col"),
            P("row", "col"),
            P("col", "row"),
            P("row", "col"),
            P("row", "col"),
            P("col", "row"),
        ),
        out_specs=P(None, ("row", "col")),
        check_vma=False,
    )
```

```python
import jax
import jax.numpy as jnp
from jax import lax
from jax.experimental import pallas as pl
from jax.experimental.pallas import tpu as pltpu
from jax.sharding import PartitionSpec as P

D = 6144
QUERY_LEN = 256
QUERIES = 8
DAMPING = 0.01

ROWS = 8
COLS = 16
TILE_I = D // ROWS
TILE_J = D // COLS
TOKENS = QUERIES * QUERY_LEN
TRAIN = 2560
BLOCK = TRAIN // 8
OWNED = TRAIN // (ROWS * COLS)

CHUNKS = 4
PER_CHUNK = QUERIES // CHUNKS
CHUNK_TOKENS = PER_CHUNK * QUERY_LEN
PIECE = CHUNK_TOKENS // 4
HALF = PIECE // 2

EVERY = 1
LAST = 4

MESH = pl.DeviceIdType.MESH
BF16 = jnp.bfloat16
F32 = jnp.float32

AG_A, AG_G, AG_TA, AG_TG = 0, 9, 18, 27
SIB_A, SIB_G, SIB_TG = 36, 44, 52
SIB_BASIS = 60
REDUCE = 61
PER_REDUCE = 10
FIRST = REDUCE + 2 * CHUNKS * PER_REDUCE
SECOND = FIRST + ROWS - 1
N_SEMS = SECOND + COLS - 1


def kernel(
    qa_ref, qg_ref, ab_ref, gb_ref, eig_ref, ta_ref, tg_ref, out_ref,
    qa, qg, ab, gb, rcp, ta, tg, part, rot_a, rot_g, near, mid, mine, other,
    panels, acc, blocks, first, split, second, local, sent, got,
):
    r = lax.axis_index("row")
    c = lax.axis_index("col")
    xl, y = r // 4, r % 4
    xh, z, k = c // 8, (c // 2) % 4, c % 2
    sib = (r, c + 1 - 2 * k)

    class Group:
        pass

    row_g, col_g = Group(), Group()
    row_g.p, row_g.u = xl, y
    row_g.up, row_g.dn = (xl * 4 + (y + 1) % 4, c), (xl * 4 + (y + 3) % 4, c)
    row_g.pair = ((1 - xl) * 4 + y, c)
    col_g.p, col_g.u = xh, z
    col_g.up = (r, xh * 8 + ((z + 1) % 4) * 2 + k)
    col_g.dn = (r, xh * 8 + ((z + 3) % 4) * 2 + k)
    col_g.pair = (r, (1 - xh) * 8 + z * 2 + k)

    def remote(src, dst, i, dev):
        return pltpu.make_async_remote_copy(
            src_ref=src, dst_ref=dst, send_sem=sent.at[i], recv_sem=got.at[i],
            device_id=dev, device_id_type=MESH,
        )

    def lanes(core):
        return pl.ds(pl.multiple_of(core * TILE_J, TILE_J), TILE_J)

    def rows_of(ref, core, size):
        def view(slot, lo, n):
            return ref.at[slot, pl.ds(pl.multiple_of(core * size + lo, 16), n)]

        return view

    def lanes_of(ref, core):
        def view(slot, lo, n):
            return ref.at[slot, pl.ds(lo, n), lanes(core)]

        return view

    def whole(ref):
        def view(slot, lo, n):
            return ref.at[slot, pl.ds(lo, n)]

        return view

    class Gather:
        def __init__(self, g, src, view, view_sib, n, base, sib_base):
            self.g, self.src, self.view, self.view_sib = g, src, view, view_sib
            self.n, self.base, self.sib_base = n, base, sib_base
            p, u = g.p, g.u
            self.own, self.q1 = p * 4 + u, (1 - p) * 4 + u
            m, o, w = (u + 3) % 4, (u + 1) % 4, (u + 2) % 4
            self.low = (p * 4 + m, (1 - p) * 4 + m)
            self.high = (p * 4 + o, (1 - p) * 4 + o)
            self.far = (p * 4 + w, (1 - p) * 4 + w)

        def full(self, slot):
            return self.view(slot, 0, self.n)

        def half(self, slot, h):
            return self.view(slot, h * (self.n // 2), self.n // 2)

        def copies(self, stage):
            g, b = self.g, self.base
            if stage == "pair":
                return [(self.src, self.full(self.own), b, g.pair)]
            if stage == "near0":
                return [
                    (self.src, self.full(self.own), b + 1, g.up),
                    (self.src, self.full(self.own), b + 2, g.dn),
                ]
            if stage == "near1":
                v = self.full(self.q1)
                return [(v, v, b + 3, g.up), (v, v, b + 4, g.dn)]
            i = 0 if stage == "far0" else 1
            lo, hi = self.half(self.low[i], 0), self.half(self.high[i], 1)
            return [(lo, lo, b + 5 + 2 * i, g.up), (hi, hi, b + 6 + 2 * i, g.dn)]

        def start(self, stage):
            for a in self.copies(stage):
                remote(*a).start()

        def wait_send(self):
            for stage in ("pair", "near0", "near1", "far0", "far1"):
                for a in self.copies(stage):
                    remote(*a).wait_send()

        def wait(self, stage):
            b, g = self.base, self.g
            if stage == "pair":
                got_ = [(self.full(self.q1), b, g.pair)]
            elif stage in ("near0", "near1"):
                i = 0 if stage == "near0" else 1
                got_ = [
                    (self.full(self.low[i]), b + 1 + 2 * i, g.dn),
                    (self.full(self.high[i]), b + 2 + 2 * i, g.up),
                ]
            else:
                i = 0 if stage == "far0" else 1
                got_ = [
                    (self.half(self.far[i], 0), b + 5 + 2 * i, g.dn),
                    (self.half(self.far[i], 1), b + 6 + 2 * i, g.up),
                ]
            for v, i, dev in got_:
                remote(v, v, i, dev).wait_recv()

        def slots(self):
            return (
                self.own, self.q1, self.low[0], self.high[0],
                self.low[1], self.high[1], self.far[0], self.far[1],
            )

        def sib_copy(self, j):
            slot = self.slots()[j]
            src = self.src if j == 0 else self.full(slot)
            return remote(src, self.full(slot), self.sib_base + j, sib)

        def sib_start(self, *js):
            for j in js:
                self.sib_copy(j).start()

        def sib_wait(self):
            for j, slot in enumerate(self.slots()):
                v = self.view_sib(slot, 0, self.n)
                remote(v, v, self.sib_base + j, sib).wait_recv()

        def sib_wait_send(self):
            for j in range(8):
                self.sib_copy(j).wait_send()

    half_q, half_t = QUERY_LEN // 2, BLOCK // 2
    g_qa = Gather(col_g, qa_ref, rows_of(qa, k, half_q), rows_of(qa, 1 - k, half_q), half_q, AG_A, SIB_A)
    g_qg = Gather(row_g, qg_ref, lanes_of(qg, k), lanes_of(qg, 1 - k), QUERY_LEN, AG_G, SIB_G)
    g_ta = Gather(row_g, ta_ref, whole(ta), None, BLOCK, AG_TA, None)
    g_tg = Gather(col_g, tg_ref, rows_of(tg, k, half_t), rows_of(tg, 1 - k, half_t), half_t, AG_TG, SIB_TG)
    queries, trains = (g_qa, g_qg), (g_ta, g_tg)

    copies = [
        pltpu.make_async_copy(eig_ref, rcp, local.at[0]),
        pltpu.make_async_copy(qa_ref, g_qa.full(g_qa.own), local.at[1]),
        pltpu.make_async_copy(qg_ref, g_qg.full(g_qg.own), local.at[2]),
        pltpu.make_async_copy(ab_ref, ab, local.at[3]),
        pltpu.make_async_copy(
            gb_ref.at[:, lanes(k)], gb.at[pl.ds(pl.multiple_of(k * TILE_J, TILE_J), TILE_J)], local.at[4]
        ),
        pltpu.make_async_copy(ta_ref, g_ta.full(g_ta.own), local.at[5]),
        pltpu.make_async_copy(tg_ref, g_tg.full(g_tg.own), local.at[6]),
    ]

    barrier = pltpu.get_barrier_semaphore()
    row_peers = [((r + d) % ROWS, c) for d in range(1, ROWS)]
    col_peers = [(r, (c + d) % COLS) for d in range(1, COLS)]
    for dev in row_peers + col_peers:
        pl.semaphore_signal(barrier, inc=1, device_id=dev, device_id_type=MESH)
    for cp in copies:
        cp.start()
    pl.semaphore_wait(barrier, ROWS + COLS - 2)

    def train_near0():
        for g in trains:
            g.wait("near0")
            g.start("far0")
        g_tg.sib_start(2, 3)

    for g in queries:
        g.start("pair")
    for g in queries:
        g.start("near0")
        g.sib_start(0)
    own_basis = gb.at[pl.ds(pl.multiple_of(k * TILE_J, TILE_J), TILE_J)]
    sib_basis = gb.at[pl.ds(pl.multiple_of((1 - k) * TILE_J, TILE_J), TILE_J)]
    basis_copy = remote(gb_ref.at[:, lanes(1 - k)], own_basis, SIB_BASIS, sib)
    basis_copy.start()
    for g in trains:
        g.start("near0")
    g_tg.sib_start(0)

    copies[0].wait()
    rcp[...] = 1.0 / (QUERY_LEN * (rcp[...] + DAMPING))

    for g in queries:
        g.wait("near0")
        g.start("far0")
        g.sib_start(2, 3)
    for g in queries:
        g.wait("pair")
        g.start("near1")
        g.sib_start(1)
    for g in trains:
        g.start("pair")
    train_near0()
    for g in queries:
        g.wait("near1")
        g.start("far1")
        g.sib_start(4, 5)
    for g in queries:
        g.wait("far0")
        g.wait("far1")
        g.sib_start(6, 7)
    for g in queries:
        g.sib_wait()
    remote(sib_basis, sib_basis, SIB_BASIS, sib).wait_recv()
    for cp in copies[1:]:
        cp.wait()

    kinds = ((0, row_g), (1, col_g))

    def sem(t, ch, j):
        return REDUCE + (ch * 2 + t) * PER_REDUCE + j

    def rows(ch, v, lo=0, n=PIECE):
        return pl.ds(pl.multiple_of(ch * CHUNK_TOKENS + v * PIECE + lo, 16), n)

    def rotated(t, ds):
        if t == 0:
            return rot_a.at[ds]
        return rot_g.at[ds, lanes(k)]

    def at(g, d):
        return (g.u + d) % 4

    def reduce_copies(t, g, ch, step):
        if step == 1:
            v = at(g, 2)
            return [
                (part.at[t, rows(ch, v, 0, HALF)], near.at[t, ch, 0], sem(t, ch, 0), g.up),
                (part.at[t, rows(ch, v, HALF, HALF)], near.at[t, ch, 1], sem(t, ch, 1), g.dn),
            ]
        if step == 2:
            return [
                (part.at[t, rows(ch, at(g, 1))], mid.at[t, ch, 0], sem(t, ch, 2), g.up),
                (part.at[t, rows(ch, at(g, 3))], mid.at[t, ch, 1], sem(t, ch, 3), g.dn),
            ]
        if step == 3:
            return [(mine.at[t, ch], other.at[t, ch], sem(t, ch, 4), g.pair)]
        if step == 4:
            v = rotated(t, rows(ch, g.u))
            return [(v, v, sem(t, ch, 5), g.up), (v, v, sem(t, ch, 6), g.dn)]
        lo = rotated(t, rows(ch, at(g, 3), 0, HALF))
        hi = rotated(t, rows(ch, at(g, 1), HALF, HALF))
        return [(lo, lo, sem(t, ch, 7), g.up), (hi, hi, sem(t, ch, 8), g.dn)]

    def reduce_start(t, g, ch, step):
        for a in reduce_copies(t, g, ch, step):
            remote(*a).start()

    def landed(v, i, dev):
        remote(v, v, i, dev).wait_recv()

    def chunk_rows(ch):
        return pl.ds(pl.multiple_of(ch * CHUNK_TOKENS, 16), CHUNK_TOKENS)

    def sib_rot(ch):
        v = rot_g.at[chunk_rows(ch), lanes(k)]
        return remote(v, v, sem(1, ch, 9), sib)

    def partials(ch):
        ds = chunk_rows(ch)
        of = pl.ds(ch * PER_CHUNK, PER_CHUNK)
        for t, ref, basis in ((0, qa, ab), (1, qg, gb)):
            part[t, ds] = jnp.dot(
                ref[of].reshape(CHUNK_TOKENS, TILE_I), basis[...], preferred_element_type=F32
            ).astype(BF16)
        for t, g in kinds:
            reduce_start(t, g, ch, 1)

    def step2(ch):
        for t, g in kinds:
            landed(near.at[t, ch, 0], sem(t, ch, 0), g.dn)
            ds = rows(ch, at(g, 1), 0, HALF)
            part[t, ds] = (part[t, ds].astype(F32) + near[t, ch, 0].astype(F32)).astype(BF16)
            landed(near.at[t, ch, 1], sem(t, ch, 1), g.up)
            ds = rows(ch, at(g, 3), HALF, HALF)
            part[t, ds] = (part[t, ds].astype(F32) + near[t, ch, 1].astype(F32)).astype(BF16)
            reduce_start(t, g, ch, 2)

    def step3(ch):
        for t, g in kinds:
            landed(mid.at[t, ch, 0], sem(t, ch, 2), g.dn)
            landed(mid.at[t, ch, 1], sem(t, ch, 3), g.up)
            total = part[t, rows(ch, g.u)].astype(F32) + mid[t, ch, 0].astype(F32) + mid[t, ch, 1].astype(F32)
            mine[t, ch] = total.astype(BF16)
            reduce_start(t, g, ch, 3)

    def step4(ch):
        for t, g in kinds:
            landed(other.at[t, ch], sem(t, ch, 4), g.pair)
            total = (mine[t, ch].astype(F32) + other[t, ch].astype(F32)).astype(BF16)
            if t == 0:
                rot_a[rows(ch, g.u)] = total
            else:
                rot_g[rows(ch, g.u), lanes(k)] = total
            reduce_start(t, g, ch, 4)

    def step5(ch):
        for t, g in kinds:
            landed(rotated(t, rows(ch, at(g, 3))), sem(t, ch, 5), g.dn)
            landed(rotated(t, rows(ch, at(g, 1))), sem(t, ch, 6), g.up)
            reduce_start(t, g, ch, 5)

    def step6(ch):
        for t, g in reversed(kinds):
            landed(rotated(t, rows(ch, at(g, 2), 0, HALF)), sem(t, ch, 7), g.dn)
            landed(rotated(t, rows(ch, at(g, 2), HALF, HALF)), sem(t, ch, 8), g.up)
            if t == 1:
                sib_rot(ch).start()

    def make_panels(ch):
        v = rot_g.at[chunk_rows(ch), lanes(1 - k)]
        landed(v, sem(1, ch, 9), sib)
        for i in range(PER_CHUNK):
            ds = pl.ds(pl.multiple_of((ch * PER_CHUNK + i) * QUERY_LEN, QUERY_LEN), QUERY_LEN)
            outer = lax.dot_general(
                rot_g[ds], rot_a[ds], (((0,), (0,)), ((), ())), preferred_element_type=F32
            )
            panels[ch % 2, :, pl.ds(i * TILE_J, TILE_J)] = (outer * rcp[...]).astype(BF16)

    def score(ch, h):
        q_of = lax.broadcasted_iota(jnp.int32, (QUERIES, PER_CHUNK * 128), 0)
        lane = lax.broadcasted_iota(jnp.int32, (QUERIES, PER_CHUNK * 128), 1)
        pick = jnp.where(q_of == ch * PER_CHUNK + lane // 128, 1.0, 0.0).astype(BF16)

        mapped = jnp.dot(
            tg[pl.ds(4 * h, 4)].reshape(4 * BLOCK, TILE_I), panels[ch % 2], preferred_element_type=F32
        )
        acts = ta[pl.ds(4 * h, 4)].reshape(4 * BLOCK, TILE_J).astype(F32)
        sums = []
        for i in range(PER_CHUNK):
            total = None
            for j in range(TILE_J // 128):
                term = mapped[:, i * TILE_J + j * 128 : i * TILE_J + (j + 1) * 128] * acts[:, j * 128 : (j + 1) * 128]
                total = term if total is None else total + term
            sums.append(total.astype(BF16))
        lanes_sum = sums[0] if PER_CHUNK == 1 else jnp.concatenate(sums, axis=1)
        acc[h] += lax.dot_general(
            pick, lanes_sum, (((1,), (1,)), ((), ())), preferred_element_type=F32
        )

    acc[...] = jnp.zeros_like(acc)

    def slot(w, carry):
        def when(step, f):
            ch = (w - step) // EVERY

            @pl.when((w >= step) & (w - step == ch * EVERY) & (ch < CHUNKS))
            def _():
                f(ch)

        def at_slot(n, f):
            pl.when(w == n)(f)

        when(4, make_panels)
        when(0, partials)
        at_slot(0, train_pair)
        when(3, step5)
        at_slot(1, train_near1)
        at_slot(2, train_far)
        at_slot(4, g_tg.sib_wait)
        when(4, lambda ch: score(ch, 0))
        when(1, step3)
        when(2, step4)
        when(4, lambda ch: score(ch, 1))
        when(0, step2)
        when(3, step6)
        return carry

    def train_pair():
        for g in trains:
            g.wait("pair")
            g.start("near1")
        g_tg.sib_start(1)

    def train_near1():
        for g in trains:
            g.wait("near1")
            g.start("far1")
        g_tg.sib_start(4, 5)

    def train_far():
        for g in trains:
            g.wait("far0")
            g.wait("far1")
        g_tg.sib_start(6, 7)

    lax.fori_loop(0, (CHUNKS - 1) * EVERY + LAST + 1, slot, 0)

    for j in range(ROWS):
        blocks[j] = acc[j // 4, :, (j % 4) * BLOCK : (j % 4 + 1) * BLOCK]

    def to_row(d):
        peer = (r + d) % ROWS
        return remote(blocks.at[peer], first.at[d - 1], FIRST + d - 1, (peer, c))

    for d in range(1, ROWS):
        to_row(d).start()
    total = blocks[r]
    for d in range(1, ROWS):
        landed(first.at[d - 1], FIRST + d - 1, ((r + ROWS - d) % ROWS, c))
        total = total + first[d - 1]
    total = total / D
    for j in range(COLS):
        split[j] = total[:, j * OWNED : (j + 1) * OWNED]

    def to_col(d):
        peer = (c + d) % COLS
        return remote(split.at[peer], second.at[d - 1], SECOND + d - 1, (r, peer))

    for d in range(1, COLS):
        to_col(d).start()
    total = split[c]
    for d in range(1, COLS):
        landed(second.at[d - 1], SECOND + d - 1, (r, (c + COLS - d) % COLS))
        total = total + second[d - 1]
    out_ref[...] = total

    for g in queries + trains:
        g.wait_send()
    for g in (g_qa, g_qg, g_tg):
        g.sib_wait_send()
    basis_copy.wait_send()

    def drain(ch, carry):
        for t, g in kinds:
            for step in range(1, 6):
                for a in reduce_copies(t, g, ch, step):
                    remote(*a).wait_send()
        sib_rot(ch).wait_send()
        return carry

    lax.fori_loop(0, CHUNKS, drain, 0)
    for d in range(1, ROWS):
        to_row(d).wait_send()
    for d in range(1, COLS):
        to_col(d).wait_send()


def shards(*args):
    any_spec = pl.BlockSpec(memory_space=pl.ANY)
    vmem = pltpu.VMEM
    return pl.pallas_call(
        kernel,
        out_shape=jax.ShapeDtypeStruct((QUERIES, OWNED), F32),
        in_specs=[any_spec] * 7,
        out_specs=pl.BlockSpec(memory_space=pltpu.VMEM),
        scratch_shapes=[
            vmem((8, QUERY_LEN, TILE_I), BF16),
            vmem((8, QUERY_LEN, 2 * TILE_J), BF16),
            vmem((TILE_I, TILE_J), BF16),
            vmem((2 * TILE_J, TILE_J), BF16),
            vmem((TILE_I, TILE_J), F32),
            vmem((8, BLOCK, TILE_J), BF16),
            vmem((8, BLOCK, TILE_I), BF16),
            vmem((2, TOKENS, TILE_J), BF16),
            vmem((TOKENS, TILE_J), BF16),
            vmem((TOKENS, TILE_I), BF16),
            vmem((2, CHUNKS, 2, HALF, TILE_J), BF16),
            vmem((2, CHUNKS, 2, PIECE, TILE_J), BF16),
            vmem((2, CHUNKS, PIECE, TILE_J), BF16),
            vmem((2, CHUNKS, PIECE, TILE_J), BF16),
            vmem((2, TILE_I, PER_CHUNK * TILE_J), BF16),
            vmem((2, QUERIES, 4 * BLOCK), F32),
            vmem((ROWS, QUERIES, BLOCK), F32),
            vmem((ROWS - 1, QUERIES, BLOCK), F32),
            vmem((COLS, QUERIES, OWNED), F32),
            vmem((COLS - 1, QUERIES, OWNED), F32),
            pltpu.SemaphoreType.DMA((7,)),
            pltpu.SemaphoreType.DMA((N_SEMS,)),
            pltpu.SemaphoreType.DMA((N_SEMS,)),
        ],
        compiler_params=pltpu.CompilerParams(
            collective_id=0, has_side_effects=True, vmem_limit_bytes=62 * 1024 * 1024
        ),
        name="influence",
    )(*args)


def solution(mesh):
    return jax.shard_map(
        shards,
        mesh=mesh,
        in_specs=(
            P("col", "row"),
            P("row", "col"),
            P("row", "col"),
            P("col", "row"),
            P("row", "col"),
            P("row", "col"),
            P("col", "row"),
        ),
        out_specs=P(None, ("row", "col")),
        check_vma=False,
    )
```

```python
import jax
import jax.numpy as jnp
from jax import lax
from jax.experimental import pallas as pl
from jax.experimental.pallas import tpu as pltpu
from jax.sharding import PartitionSpec as P

D = 6144
QUERY_LEN = 256
QUERIES = 8
DAMPING = 0.01

ROWS = 8
COLS = 16
TILE_I = D // ROWS
TILE_J = D // COLS
TOKENS = QUERIES * QUERY_LEN
TRAIN = 2560
BLOCK = TRAIN // 8
OWNED = TRAIN // (ROWS * COLS)

CHUNKS = 4
PER_CHUNK = QUERIES // CHUNKS
CHUNK_TOKENS = PER_CHUNK * QUERY_LEN
PIECE = CHUNK_TOKENS // 4
HALF = PIECE // 2

ORDER = (
    "q0", "q1", "t0", "tp", "qn1", "qf0", "qf1", "tn1", "qe", "P0", "P1", "P3", "20", "21", "P2", "30", "tf1", "22", "31", "23", "40", "32", "tf0", "50", "41", "33", "42", "60", "te", "51", "N0", "tw", "S0", "52", "43", "61", "T0", "N1", "62", "S1", "53", "T1", "N2", "S2", "63", "T2", "N3", "S3", "T3",
)

MESH = pl.DeviceIdType.MESH
BF16 = jnp.bfloat16
F32 = jnp.float32

AG_A, AG_G, AG_TA, AG_TG = 0, 9, 18, 27
SIB_A, SIB_G, SIB_TG = 36, 44, 52
SIB_BASIS = 60
REDUCE = 61
PER_REDUCE = 10
FIRST = REDUCE + 2 * CHUNKS * PER_REDUCE
SECOND = FIRST + ROWS - 1
N_SEMS = SECOND + COLS - 1


def kernel(
    qa_ref, qg_ref, ab_ref, gb_ref, eig_ref, ta_ref, tg_ref, out_ref,
    qa, qg, ab, gb, rcp, ta, tg, part, rot_a, rot_g, near, mid, mine, other,
    panels, acc, blocks, first, split, second, local, sent, got,
):
    r = lax.axis_index("row")
    c = lax.axis_index("col")
    xl, y = r // 4, r % 4
    xh, z, k = c // 8, (c // 2) % 4, c % 2
    sib = (r, c + 1 - 2 * k)

    class Group:
        pass

    row_g, col_g = Group(), Group()
    row_g.p, row_g.u = xl, y
    row_g.up, row_g.dn = (xl * 4 + (y + 1) % 4, c), (xl * 4 + (y + 3) % 4, c)
    row_g.pair = ((1 - xl) * 4 + y, c)
    col_g.p, col_g.u = xh, z
    col_g.up = (r, xh * 8 + ((z + 1) % 4) * 2 + k)
    col_g.dn = (r, xh * 8 + ((z + 3) % 4) * 2 + k)
    col_g.pair = (r, (1 - xh) * 8 + z * 2 + k)

    def remote(src, dst, i, dev):
        return pltpu.make_async_remote_copy(
            src_ref=src, dst_ref=dst, send_sem=sent.at[i], recv_sem=got.at[i],
            device_id=dev, device_id_type=MESH,
        )

    def lanes(core):
        return pl.ds(pl.multiple_of(core * TILE_J, TILE_J), TILE_J)

    def rows_of(ref, core, size):
        def view(slot, lo, n):
            return ref.at[slot, pl.ds(pl.multiple_of(core * size + lo, 16), n)]

        return view

    def lanes_of(ref, core):
        def view(slot, lo, n):
            return ref.at[slot, pl.ds(lo, n), lanes(core)]

        return view

    def whole(ref):
        def view(slot, lo, n):
            return ref.at[slot, pl.ds(lo, n)]

        return view

    class Gather:
        def __init__(self, g, src, view, view_sib, n, base, sib_base):
            self.g, self.src, self.view, self.view_sib = g, src, view, view_sib
            self.n, self.base, self.sib_base = n, base, sib_base
            p, u = g.p, g.u
            self.own, self.q1 = p * 4 + u, (1 - p) * 4 + u
            m, o, w = (u + 3) % 4, (u + 1) % 4, (u + 2) % 4
            self.low = (p * 4 + m, (1 - p) * 4 + m)
            self.high = (p * 4 + o, (1 - p) * 4 + o)
            self.far = (p * 4 + w, (1 - p) * 4 + w)

        def full(self, slot):
            return self.view(slot, 0, self.n)

        def half(self, slot, h):
            return self.view(slot, h * (self.n // 2), self.n // 2)

        def copies(self, stage):
            g, b = self.g, self.base
            if stage == "pair":
                return [(self.src, self.full(self.own), b, g.pair)]
            if stage == "near0":
                return [
                    (self.src, self.full(self.own), b + 1, g.up),
                    (self.src, self.full(self.own), b + 2, g.dn),
                ]
            if stage == "near1":
                v = self.full(self.q1)
                return [(v, v, b + 3, g.up), (v, v, b + 4, g.dn)]
            i = 0 if stage == "far0" else 1
            lo, hi = self.half(self.low[i], 0), self.half(self.high[i], 1)
            return [(lo, lo, b + 5 + 2 * i, g.up), (hi, hi, b + 6 + 2 * i, g.dn)]

        def start(self, stage):
            for a in self.copies(stage):
                remote(*a).start()

        def wait_send(self):
            for stage in ("pair", "near0", "near1", "far0", "far1"):
                for a in self.copies(stage):
                    remote(*a).wait_send()

        def wait(self, stage):
            b, g = self.base, self.g
            if stage == "pair":
                got_ = [(self.full(self.q1), b, g.pair)]
            elif stage in ("near0", "near1"):
                i = 0 if stage == "near0" else 1
                got_ = [
                    (self.full(self.low[i]), b + 1 + 2 * i, g.dn),
                    (self.full(self.high[i]), b + 2 + 2 * i, g.up),
                ]
            else:
                i = 0 if stage == "far0" else 1
                got_ = [
                    (self.half(self.far[i], 0), b + 5 + 2 * i, g.dn),
                    (self.half(self.far[i], 1), b + 6 + 2 * i, g.up),
                ]
            for v, i, dev in got_:
                remote(v, v, i, dev).wait_recv()

        def slots(self):
            return (
                self.own, self.q1, self.low[0], self.high[0],
                self.low[1], self.high[1], self.far[0], self.far[1],
            )

        def sib_copy(self, j):
            slot = self.slots()[j]
            src = self.src if j == 0 else self.full(slot)
            return remote(src, self.full(slot), self.sib_base + j, sib)

        def sib_start(self, *js):
            for j in js:
                self.sib_copy(j).start()

        def sib_wait(self):
            for j, slot in enumerate(self.slots()):
                v = self.view_sib(slot, 0, self.n)
                remote(v, v, self.sib_base + j, sib).wait_recv()

        def sib_wait_send(self):
            for j in range(8):
                self.sib_copy(j).wait_send()

    half_q, half_t = QUERY_LEN // 2, BLOCK // 2
    g_qa = Gather(col_g, qa_ref, rows_of(qa, k, half_q), rows_of(qa, 1 - k, half_q), half_q, AG_A, SIB_A)
    g_qg = Gather(row_g, qg_ref, lanes_of(qg, k), lanes_of(qg, 1 - k), QUERY_LEN, AG_G, SIB_G)
    g_ta = Gather(row_g, ta_ref, whole(ta), None, BLOCK, AG_TA, None)
    g_tg = Gather(col_g, tg_ref, rows_of(tg, k, half_t), rows_of(tg, 1 - k, half_t), half_t, AG_TG, SIB_TG)
    queries, trains = (g_qa, g_qg), (g_ta, g_tg)

    copies = [
        pltpu.make_async_copy(eig_ref, rcp, local.at[0]),
        pltpu.make_async_copy(qa_ref, g_qa.full(g_qa.own), local.at[1]),
        pltpu.make_async_copy(qg_ref, g_qg.full(g_qg.own), local.at[2]),
        pltpu.make_async_copy(ab_ref, ab, local.at[3]),
        pltpu.make_async_copy(
            gb_ref.at[:, lanes(k)], gb.at[pl.ds(pl.multiple_of(k * TILE_J, TILE_J), TILE_J)], local.at[4]
        ),
        pltpu.make_async_copy(ta_ref, g_ta.full(g_ta.own), local.at[5]),
        pltpu.make_async_copy(tg_ref, g_tg.full(g_tg.own), local.at[6]),
    ]

    barrier = pltpu.get_barrier_semaphore()
    row_peers = [((r + d) % ROWS, c) for d in range(1, ROWS)]
    col_peers = [(r, (c + d) % COLS) for d in range(1, COLS)]
    for dev in row_peers + col_peers:
        pl.semaphore_signal(barrier, inc=1, device_id=dev, device_id_type=MESH)
    for cp in copies:
        cp.start()
    pl.semaphore_wait(barrier, ROWS + COLS - 2)

    own_basis = gb.at[pl.ds(pl.multiple_of(k * TILE_J, TILE_J), TILE_J)]
    sib_basis = gb.at[pl.ds(pl.multiple_of((1 - k) * TILE_J, TILE_J), TILE_J)]
    basis_copy = remote(gb_ref.at[:, lanes(1 - k)], own_basis, SIB_BASIS, sib)

    def query_pair():
        for g in queries:
            g.start("pair")

    def query_own():
        for g in queries:
            g.start("near0")
            g.sib_start(0)
        basis_copy.start()

    def train_own():
        for g in trains:
            g.start("near0")
        g_tg.sib_start(0)
        copies[0].wait()
        rcp[...] = 1.0 / (QUERY_LEN * (rcp[...] + DAMPING))

    def query_near0():
        for g in queries:
            g.wait("near0")
            g.start("far0")
            g.sib_start(2, 3)

    def query_pair_in():
        for g in queries:
            g.wait("pair")
            g.start("near1")
            g.sib_start(1)

    def train_pair_out():
        for g in trains:
            g.start("pair")

    def train_near0():
        for g in trains:
            g.wait("near0")
            g.start("far0")
        g_tg.sib_start(2, 3)

    def query_near1():
        for g in queries:
            g.wait("near1")
            g.start("far1")
            g.sib_start(4, 5)

    def query_far():
        for g in queries:
            g.wait("far0")
            g.wait("far1")
            g.sib_start(6, 7)
        for g in queries:
            g.sib_wait()
        remote(sib_basis, sib_basis, SIB_BASIS, sib).wait_recv()
        for cp in copies[1:]:
            cp.wait()

    kinds = ((0, row_g), (1, col_g))

    def sem(t, ch, j):
        return REDUCE + (ch * 2 + t) * PER_REDUCE + j

    def rows(ch, v, lo=0, n=PIECE):
        return pl.ds(pl.multiple_of(ch * CHUNK_TOKENS + v * PIECE + lo, 16), n)

    def rotated(t, ds):
        if t == 0:
            return rot_a.at[ds]
        return rot_g.at[ds, lanes(k)]

    def at(g, d):
        return (g.u + d) % 4

    def reduce_copies(t, g, ch, step):
        if step == 1:
            v = at(g, 2)
            return [
                (part.at[t, rows(ch, v, 0, HALF)], near.at[t, ch, 0], sem(t, ch, 0), g.up),
                (part.at[t, rows(ch, v, HALF, HALF)], near.at[t, ch, 1], sem(t, ch, 1), g.dn),
            ]
        if step == 2:
            return [
                (part.at[t, rows(ch, at(g, 1))], mid.at[t, ch, 0], sem(t, ch, 2), g.up),
                (part.at[t, rows(ch, at(g, 3))], mid.at[t, ch, 1], sem(t, ch, 3), g.dn),
            ]
        if step == 3:
            return [(mine.at[t, ch], other.at[t, ch], sem(t, ch, 4), g.pair)]
        if step == 4:
            v = rotated(t, rows(ch, g.u))
            return [(v, v, sem(t, ch, 5), g.up), (v, v, sem(t, ch, 6), g.dn)]
        lo = rotated(t, rows(ch, at(g, 3), 0, HALF))
        hi = rotated(t, rows(ch, at(g, 1), HALF, HALF))
        return [(lo, lo, sem(t, ch, 7), g.up), (hi, hi, sem(t, ch, 8), g.dn)]

    def reduce_start(t, g, ch, step):
        for a in reduce_copies(t, g, ch, step):
            remote(*a).start()

    def landed(v, i, dev):
        remote(v, v, i, dev).wait_recv()

    def chunk_rows(ch):
        return pl.ds(pl.multiple_of(ch * CHUNK_TOKENS, 16), CHUNK_TOKENS)

    def sib_rot(ch):
        v = rot_g.at[chunk_rows(ch), lanes(k)]
        return remote(v, v, sem(1, ch, 9), sib)

    def partials(ch):
        ds = chunk_rows(ch)
        of = pl.ds(ch * PER_CHUNK, PER_CHUNK)
        for t, ref, basis in ((0, qa, ab), (1, qg, gb)):
            part[t, ds] = jnp.dot(
                ref[of].reshape(CHUNK_TOKENS, TILE_I), basis[...], preferred_element_type=F32
            ).astype(BF16)
        for t, g in kinds:
            reduce_start(t, g, ch, 1)

    def step2(ch):
        for t, g in kinds:
            landed(near.at[t, ch, 0], sem(t, ch, 0), g.dn)
            ds = rows(ch, at(g, 1), 0, HALF)
            part[t, ds] = (part[t, ds].astype(F32) + near[t, ch, 0].astype(F32)).astype(BF16)
            landed(near.at[t, ch, 1], sem(t, ch, 1), g.up)
            ds = rows(ch, at(g, 3), HALF, HALF)
            part[t, ds] = (part[t, ds].astype(F32) + near[t, ch, 1].astype(F32)).astype(BF16)
            reduce_start(t, g, ch, 2)

    def step3(ch):
        for t, g in kinds:
            landed(mid.at[t, ch, 0], sem(t, ch, 2), g.dn)
            landed(mid.at[t, ch, 1], sem(t, ch, 3), g.up)
            total = part[t, rows(ch, g.u)].astype(F32) + mid[t, ch, 0].astype(F32) + mid[t, ch, 1].astype(F32)
            mine[t, ch] = total.astype(BF16)
            reduce_start(t, g, ch, 3)

    def step4(ch):
        for t, g in kinds:
            landed(other.at[t, ch], sem(t, ch, 4), g.pair)
            total = (mine[t, ch].astype(F32) + other[t, ch].astype(F32)).astype(BF16)
            if t == 0:
                rot_a[rows(ch, g.u)] = total
            else:
                rot_g[rows(ch, g.u), lanes(k)] = total
            reduce_start(t, g, ch, 4)

    def step5(ch):
        for t, g in kinds:
            landed(rotated(t, rows(ch, at(g, 3))), sem(t, ch, 5), g.dn)
            landed(rotated(t, rows(ch, at(g, 1))), sem(t, ch, 6), g.up)
            reduce_start(t, g, ch, 5)

    def step6(ch):
        for t, g in reversed(kinds):
            landed(rotated(t, rows(ch, at(g, 2), 0, HALF)), sem(t, ch, 7), g.dn)
            landed(rotated(t, rows(ch, at(g, 2), HALF, HALF)), sem(t, ch, 8), g.up)
            if t == 1:
                sib_rot(ch).start()

    def make_panels(ch):
        v = rot_g.at[chunk_rows(ch), lanes(1 - k)]
        landed(v, sem(1, ch, 9), sib)
        for i in range(PER_CHUNK):
            ds = pl.ds(pl.multiple_of((ch * PER_CHUNK + i) * QUERY_LEN, QUERY_LEN), QUERY_LEN)
            outer = lax.dot_general(
                rot_g[ds], rot_a[ds], (((0,), (0,)), ((), ())), preferred_element_type=F32
            )
            panels[ch % 2, :, pl.ds(i * TILE_J, TILE_J)] = (outer * rcp[...]).astype(BF16)

    def score(ch, h):
        mapped = jnp.dot(
            tg[pl.ds(4 * h, 4)].reshape(4 * BLOCK, TILE_I), panels[ch % 2], preferred_element_type=F32
        )
        acts = ta[pl.ds(4 * h, 4)].reshape(4 * BLOCK, TILE_J).astype(F32)
        for i in range(PER_CHUNK):
            q = ch * PER_CHUNK + i
            total = None
            for j in range(TILE_J // 128):
                term = mapped[:, i * TILE_J + j * 128 : i * TILE_J + (j + 1) * 128] * acts[:, j * 128 : (j + 1) * 128]
                total = term if total is None else total + term
            acc[h, :, q : q + 1] = jnp.sum(total, axis=1, keepdims=True)

    acc[...] = jnp.zeros_like(acc)
    split[...] = jnp.zeros_like(split)

    def train_pair():
        for g in trains:
            g.wait("pair")
            g.start("near1")
        g_tg.sib_start(1)

    def train_near1():
        for g in trains:
            g.wait("near1")
            g.start("far1")
        g_tg.sib_start(4, 5)

    def train_far():
        for g in trains:
            g.wait("far0")
            g.wait("far1")
        g_tg.sib_start(6, 7)

    def train_end():
        g_tg.sib_wait()

    events = {
        "q0": query_pair, "q1": query_own, "t0": train_own, "qf0": query_near0, "qn1": query_pair_in,
        "tp": train_pair_out, "tf0": train_near0, "qf1": query_near1, "qe": query_far,
        "tn1": train_pair, "tf1": train_near1, "te": train_far, "tw": train_end,
    }
    steps = {
        "P": partials, "2": step2, "3": step3, "4": step4, "5": step5, "6": step6,
        "N": make_panels, "S": lambda ch: score(ch, 0), "T": lambda ch: score(ch, 1),
    }
    for name in ORDER:
        if name in events:
            events[name]()
        else:
            steps[name[0]](int(name[1:]))

    for h in range(2):
        turned = acc[h].T[:QUERIES]
        for j in range(4):
            blocks[4 * h + j] = turned[:, j * BLOCK : (j + 1) * BLOCK]

    def to_row(d):
        peer = (r + d) % ROWS
        return remote(blocks.at[peer], first.at[d - 1], FIRST + d - 1, (peer, c))

    for d in range(1, ROWS):
        to_row(d).start()
    total = blocks[r]
    for d in range(1, ROWS):
        landed(first.at[d - 1], FIRST + d - 1, ((r + ROWS - d) % ROWS, c))
        total = total + first[d - 1]
    total = total / D
    for j in range(COLS):
        split[j, :, :OWNED] = total[:, j * OWNED : (j + 1) * OWNED]

    def to_col(d):
        peer = (c + d) % COLS
        return remote(split.at[peer], second.at[d - 1], SECOND + d - 1, (r, peer))

    for d in range(1, COLS):
        to_col(d).start()
    total = split[c]
    for d in range(1, COLS):
        landed(second.at[d - 1], SECOND + d - 1, (r, (c + COLS - d) % COLS))
        total = total + second[d - 1]
    out_ref[...] = total[:, :OWNED]

    for g in queries + trains:
        g.wait_send()
    for g in (g_qa, g_qg, g_tg):
        g.sib_wait_send()
    basis_copy.wait_send()

    def drain(ch, carry):
        for t, g in kinds:
            for step in range(1, 6):
                for a in reduce_copies(t, g, ch, step):
                    remote(*a).wait_send()
        sib_rot(ch).wait_send()
        return carry

    lax.fori_loop(0, CHUNKS, drain, 0)
    for d in range(1, ROWS):
        to_row(d).wait_send()
    for d in range(1, COLS):
        to_col(d).wait_send()


def shards(*args):
    any_spec = pl.BlockSpec(memory_space=pl.ANY)
    vmem = pltpu.VMEM
    return pl.pallas_call(
        kernel,
        out_shape=jax.ShapeDtypeStruct((QUERIES, OWNED), F32),
        in_specs=[any_spec] * 7,
        out_specs=pl.BlockSpec(memory_space=pltpu.VMEM),
        scratch_shapes=[
            vmem((8, QUERY_LEN, TILE_I), BF16),
            vmem((8, QUERY_LEN, 2 * TILE_J), BF16),
            vmem((TILE_I, TILE_J), BF16),
            vmem((2 * TILE_J, TILE_J), BF16),
            vmem((TILE_I, TILE_J), F32),
            vmem((8, BLOCK, TILE_J), BF16),
            vmem((8, BLOCK, TILE_I), BF16),
            vmem((2, TOKENS, TILE_J), BF16),
            vmem((TOKENS, TILE_J), BF16),
            vmem((TOKENS, TILE_I), BF16),
            vmem((2, CHUNKS, 2, HALF, TILE_J), BF16),
            vmem((2, CHUNKS, 2, PIECE, TILE_J), BF16),
            vmem((2, CHUNKS, PIECE, TILE_J), BF16),
            vmem((2, CHUNKS, PIECE, TILE_J), BF16),
            vmem((2, TILE_I, PER_CHUNK * TILE_J), BF16),
            vmem((2, 4 * BLOCK, 128), F32),
            vmem((ROWS, QUERIES, BLOCK), F32),
            vmem((ROWS - 1, QUERIES, BLOCK), F32),
            vmem((COLS, QUERIES, 128), F32),
            vmem((COLS - 1, QUERIES, 128), F32),
            pltpu.SemaphoreType.DMA((7,)),
            pltpu.SemaphoreType.DMA((N_SEMS,)),
            pltpu.SemaphoreType.DMA((N_SEMS,)),
        ],
        compiler_params=pltpu.CompilerParams(
            collective_id=0, has_side_effects=True, vmem_limit_bytes=62 * 1024 * 1024
        ),
        name="influence",
    )(*args)


def solution(mesh):
    return jax.shard_map(
        shards,
        mesh=mesh,
        in_specs=(
            P("col", "row"),
            P("row", "col"),
            P("row", "col"),
            P("col", "row"),
            P("row", "col"),
            P("row", "col"),
            P("col", "row"),
        ),
        out_specs=P(None, ("row", "col")),
        check_vma=False,
    )
```

```python
import jax
import jax.numpy as jnp
from jax import lax
from jax.experimental import pallas as pl
from jax.experimental.pallas import tpu as pltpu
from jax.sharding import PartitionSpec as P

D = 6144
QUERY_LEN = 256
QUERIES = 8
DAMPING = 0.01

ROWS = 8
COLS = 16
TILE_I = D // ROWS
TILE_J = D // COLS
TOKENS = QUERIES * QUERY_LEN
TRAIN = 2560
BLOCK = TRAIN // 8
OWNED = TRAIN // (ROWS * COLS)

SIZES = (2, 2, 2, 2)
CHUNKS = len(SIZES)
STARTS = tuple(sum(SIZES[:ch]) for ch in range(CHUNKS))

ORDER = (
    "q0", "q1", "t0", "qf0", "tp", "qn1", "tf0", "qf1", "tn1", "qe", "qw", "P0", "P1", "P2",
    "20", "P3", "21", "22", "30", "23", "31", "32", "40", "tf1", "33", "50", "41", "te",
    "42", "60", "51", "N0", "43", "tw", "S0", "52", "61", "T0", "N1", "53", "S1", "62",
    "T1", "63", "N2", "S2", "T2", "N3", "S3", "T3",
)

MESH = pl.DeviceIdType.MESH
BF16 = jnp.bfloat16
F32 = jnp.float32

AG_A, AG_G, AG_TA, AG_TG = 0, 9, 18, 27
SIB_A, SIB_G, SIB_TG = 36, 44, 52
SIB_BASIS = 60
REDUCE = 61
PER_REDUCE = 10
FIRST = REDUCE + 2 * CHUNKS * PER_REDUCE
SECOND = FIRST + ROWS - 1
N_SEMS = SECOND + COLS - 1


def kernel(
    qa_ref, qg_ref, ab_ref, gb_ref, eig_ref, ta_ref, tg_ref, out_ref,
    qa, qg, ab, gb, rcp, ta, tg, part, rot_a, rot_g, near, mid, mine, other,
    panels, acc, blocks, first, split, second, local, sent, got,
):
    r = lax.axis_index("row")
    c = lax.axis_index("col")
    xl, y = r // 4, r % 4
    xh, z, k = c // 8, (c // 2) % 4, c % 2
    sib = (r, c + 1 - 2 * k)

    class Group:
        pass

    row_g, col_g = Group(), Group()
    row_g.p, row_g.u = xl, y
    row_g.up, row_g.dn = (xl * 4 + (y + 1) % 4, c), (xl * 4 + (y + 3) % 4, c)
    row_g.pair = ((1 - xl) * 4 + y, c)
    col_g.p, col_g.u = xh, z
    col_g.up = (r, xh * 8 + ((z + 1) % 4) * 2 + k)
    col_g.dn = (r, xh * 8 + ((z + 3) % 4) * 2 + k)
    col_g.pair = (r, (1 - xh) * 8 + z * 2 + k)

    def remote(src, dst, i, dev):
        return pltpu.make_async_remote_copy(
            src_ref=src, dst_ref=dst, send_sem=sent.at[i], recv_sem=got.at[i],
            device_id=dev, device_id_type=MESH,
        )

    def lanes(core):
        return pl.ds(pl.multiple_of(core * TILE_J, TILE_J), TILE_J)

    def rows_of(ref, core, size):
        def view(slot, lo, n):
            return ref.at[slot, pl.ds(pl.multiple_of(core * size + lo, 16), n)]

        return view

    def lanes_of(ref, core):
        def view(slot, lo, n):
            return ref.at[slot, pl.ds(lo, n), lanes(core)]

        return view

    def whole(ref):
        def view(slot, lo, n):
            return ref.at[slot, pl.ds(lo, n)]

        return view

    class Gather:
        def __init__(self, g, src, view, view_sib, n, base, sib_base):
            self.g, self.src, self.view, self.view_sib = g, src, view, view_sib
            self.n, self.base, self.sib_base = n, base, sib_base
            p, u = g.p, g.u
            self.own, self.q1 = p * 4 + u, (1 - p) * 4 + u
            m, o, w = (u + 3) % 4, (u + 1) % 4, (u + 2) % 4
            self.low = (p * 4 + m, (1 - p) * 4 + m)
            self.high = (p * 4 + o, (1 - p) * 4 + o)
            self.far = (p * 4 + w, (1 - p) * 4 + w)

        def full(self, slot):
            return self.view(slot, 0, self.n)

        def half(self, slot, h):
            return self.view(slot, h * (self.n // 2), self.n // 2)

        def copies(self, stage):
            g, b = self.g, self.base
            if stage == "pair":
                return [(self.src, self.full(self.own), b, g.pair)]
            if stage == "near0":
                return [
                    (self.src, self.full(self.own), b + 1, g.up),
                    (self.src, self.full(self.own), b + 2, g.dn),
                ]
            if stage == "near1":
                v = self.full(self.q1)
                return [(v, v, b + 3, g.up), (v, v, b + 4, g.dn)]
            i = 0 if stage == "far0" else 1
            lo, hi = self.half(self.low[i], 0), self.half(self.high[i], 1)
            return [(lo, lo, b + 5 + 2 * i, g.up), (hi, hi, b + 6 + 2 * i, g.dn)]

        def start(self, stage):
            for a in self.copies(stage):
                remote(*a).start()

        def wait_send(self):
            for stage in ("pair", "near0", "near1", "far0", "far1"):
                for a in self.copies(stage):
                    remote(*a).wait_send()

        def wait(self, stage):
            b, g = self.base, self.g
            if stage == "pair":
                got_ = [(self.full(self.q1), b, g.pair)]
            elif stage in ("near0", "near1"):
                i = 0 if stage == "near0" else 1
                got_ = [
                    (self.full(self.low[i]), b + 1 + 2 * i, g.dn),
                    (self.full(self.high[i]), b + 2 + 2 * i, g.up),
                ]
            else:
                i = 0 if stage == "far0" else 1
                got_ = [
                    (self.half(self.far[i], 0), b + 5 + 2 * i, g.dn),
                    (self.half(self.far[i], 1), b + 6 + 2 * i, g.up),
                ]
            for v, i, dev in got_:
                remote(v, v, i, dev).wait_recv()

        def slots(self):
            return (
                self.own, self.q1, self.low[0], self.high[0],
                self.low[1], self.high[1], self.far[0], self.far[1],
            )

        def sib_copy(self, j):
            slot = self.slots()[j]
            src = self.src if j == 0 else self.full(slot)
            return remote(src, self.full(slot), self.sib_base + j, sib)

        def sib_start(self, *js):
            for j in js:
                self.sib_copy(j).start()

        def sib_wait(self):
            for j, slot in enumerate(self.slots()):
                v = self.view_sib(slot, 0, self.n)
                remote(v, v, self.sib_base + j, sib).wait_recv()

        def sib_wait_send(self):
            for j in range(8):
                self.sib_copy(j).wait_send()

    half_q, half_t = QUERY_LEN // 2, BLOCK // 2
    g_qa = Gather(col_g, qa_ref, rows_of(qa, k, half_q), rows_of(qa, 1 - k, half_q), half_q, AG_A, SIB_A)
    g_qg = Gather(row_g, qg_ref, lanes_of(qg, k), lanes_of(qg, 1 - k), QUERY_LEN, AG_G, SIB_G)
    g_ta = Gather(row_g, ta_ref, whole(ta), None, BLOCK, AG_TA, None)
    g_tg = Gather(col_g, tg_ref, rows_of(tg, k, half_t), rows_of(tg, 1 - k, half_t), half_t, AG_TG, SIB_TG)
    queries, trains = (g_qa, g_qg), (g_ta, g_tg)

    copies = [
        pltpu.make_async_copy(eig_ref, rcp, local.at[0]),
        pltpu.make_async_copy(qa_ref, g_qa.full(g_qa.own), local.at[1]),
        pltpu.make_async_copy(qg_ref, g_qg.full(g_qg.own), local.at[2]),
        pltpu.make_async_copy(ab_ref, ab, local.at[3]),
        pltpu.make_async_copy(
            gb_ref.at[:, lanes(k)], gb.at[pl.ds(pl.multiple_of(k * TILE_J, TILE_J), TILE_J)], local.at[4]
        ),
        pltpu.make_async_copy(ta_ref, g_ta.full(g_ta.own), local.at[5]),
        pltpu.make_async_copy(tg_ref, g_tg.full(g_tg.own), local.at[6]),
    ]

    barrier = pltpu.get_barrier_semaphore()
    row_peers = [((r + d) % ROWS, c) for d in range(1, ROWS)]
    col_peers = [(r, (c + d) % COLS) for d in range(1, COLS)]
    for dev in row_peers + col_peers:
        pl.semaphore_signal(barrier, inc=1, device_id=dev, device_id_type=MESH)
    for cp in copies:
        cp.start()
    pl.semaphore_wait(barrier, ROWS + COLS - 2)

    own_basis = gb.at[pl.ds(pl.multiple_of(k * TILE_J, TILE_J), TILE_J)]
    sib_basis = gb.at[pl.ds(pl.multiple_of((1 - k) * TILE_J, TILE_J), TILE_J)]
    basis_copy = remote(gb_ref.at[:, lanes(1 - k)], own_basis, SIB_BASIS, sib)

    def query_pair():
        for g in queries:
            g.start("pair")

    def query_own():
        for g in queries:
            g.start("near0")
            g.sib_start(0)
        basis_copy.start()

    def train_own():
        for g in trains:
            g.start("near0")
        g_tg.sib_start(0)
        copies[0].wait()
        rcp[...] = 1.0 / (QUERY_LEN * (rcp[...] + DAMPING))

    def query_near0():
        for g in queries:
            g.wait("near0")
            g.start("far0")
            g.sib_start(2, 3)

    def query_pair_in():
        for g in queries:
            g.wait("pair")
            g.start("near1")
            g.sib_start(1)

    def train_pair_out():
        for g in trains:
            g.start("pair")

    def train_near0():
        for g in trains:
            g.wait("near0")
            g.start("far0")
        g_tg.sib_start(2, 3)

    def query_near1():
        for g in queries:
            g.wait("near1")
            g.start("far1")
            g.sib_start(4, 5)

    def query_far():
        for g in queries:
            g.wait("far0")
            g.wait("far1")
            g.sib_start(6, 7)

    def query_end():
        for g in queries:
            g.sib_wait()
        remote(sib_basis, sib_basis, SIB_BASIS, sib).wait_recv()
        for cp in copies[1:]:
            cp.wait()

    kinds = ((0, row_g), (1, col_g))

    def sem(t, ch, j):
        return REDUCE + (ch * 2 + t) * PER_REDUCE + j

    def piece(ch):
        return SIZES[ch] * QUERY_LEN // 4

    def rows(ch, v, h=None):
        n = piece(ch)
        lo = STARTS[ch] * QUERY_LEN + v * n
        if h is not None:
            n = n // 2
            lo = lo + h * n
        return pl.ds(pl.multiple_of(lo, 16), n)

    def quarter(ch):
        return pl.ds(STARTS[ch] * QUERY_LEN // 4, piece(ch))

    def eighth(ch):
        return pl.ds(STARTS[ch] * QUERY_LEN // 8, piece(ch) // 2)

    def rotated(t, ds):
        if t == 0:
            return rot_a.at[ds]
        return rot_g.at[ds, lanes(k)]

    def at(g, d):
        return (g.u + d) % 4

    def reduce_copies(t, g, ch, step):
        if step == 1:
            v = at(g, 2)
            return [
                (part.at[t, rows(ch, v, 0)], near.at[t, 0, eighth(ch)], sem(t, ch, 0), g.up),
                (part.at[t, rows(ch, v, 1)], near.at[t, 1, eighth(ch)], sem(t, ch, 1), g.dn),
            ]
        if step == 2:
            return [
                (part.at[t, rows(ch, at(g, 1))], mid.at[t, 0, quarter(ch)], sem(t, ch, 2), g.up),
                (part.at[t, rows(ch, at(g, 3))], mid.at[t, 1, quarter(ch)], sem(t, ch, 3), g.dn),
            ]
        if step == 3:
            return [(mine.at[t, quarter(ch)], other.at[t, quarter(ch)], sem(t, ch, 4), g.pair)]
        if step == 4:
            v = rotated(t, rows(ch, g.u))
            return [(v, v, sem(t, ch, 5), g.up), (v, v, sem(t, ch, 6), g.dn)]
        lo = rotated(t, rows(ch, at(g, 3), 0))
        hi = rotated(t, rows(ch, at(g, 1), 1))
        return [(lo, lo, sem(t, ch, 7), g.up), (hi, hi, sem(t, ch, 8), g.dn)]

    def reduce_start(t, g, ch, step):
        for a in reduce_copies(t, g, ch, step):
            remote(*a).start()

    def landed(v, i, dev):
        remote(v, v, i, dev).wait_recv()

    def chunk_rows(ch):
        return pl.ds(STARTS[ch] * QUERY_LEN, SIZES[ch] * QUERY_LEN)

    def sib_rot(ch):
        v = rot_g.at[chunk_rows(ch), lanes(k)]
        return remote(v, v, sem(1, ch, 9), sib)

    def partials(ch):
        ds = chunk_rows(ch)
        of = pl.ds(STARTS[ch], SIZES[ch])
        for t, ref, basis in ((0, qa, ab), (1, qg, gb)):
            part[t, ds] = jnp.dot(
                ref[of].reshape(SIZES[ch] * QUERY_LEN, TILE_I), basis[...], preferred_element_type=F32
            ).astype(BF16)
        for t, g in kinds:
            reduce_start(t, g, ch, 1)

    def step2(ch):
        for t, g in kinds:
            landed(near.at[t, 0, eighth(ch)], sem(t, ch, 0), g.dn)
            ds = rows(ch, at(g, 1), 0)
            part[t, ds] = (part[t, ds].astype(F32) + near[t, 0, eighth(ch)].astype(F32)).astype(BF16)
            landed(near.at[t, 1, eighth(ch)], sem(t, ch, 1), g.up)
            ds = rows(ch, at(g, 3), 1)
            part[t, ds] = (part[t, ds].astype(F32) + near[t, 1, eighth(ch)].astype(F32)).astype(BF16)
            reduce_start(t, g, ch, 2)

    def step3(ch):
        for t, g in kinds:
            landed(mid.at[t, 0, quarter(ch)], sem(t, ch, 2), g.dn)
            landed(mid.at[t, 1, quarter(ch)], sem(t, ch, 3), g.up)
            total = part[t, rows(ch, g.u)].astype(F32) + mid[t, 0, quarter(ch)].astype(F32) + mid[t, 1, quarter(ch)].astype(F32)
            mine[t, quarter(ch)] = total.astype(BF16)
            reduce_start(t, g, ch, 3)

    def step4(ch):
        for t, g in kinds:
            landed(other.at[t, quarter(ch)], sem(t, ch, 4), g.pair)
            total = (mine[t, quarter(ch)].astype(F32) + other[t, quarter(ch)].astype(F32)).astype(BF16)
            if t == 0:
                rot_a[rows(ch, g.u)] = total
            else:
                rot_g[rows(ch, g.u), lanes(k)] = total
            reduce_start(t, g, ch, 4)

    def step5(ch):
        for t, g in kinds:
            landed(rotated(t, rows(ch, at(g, 3))), sem(t, ch, 5), g.dn)
            landed(rotated(t, rows(ch, at(g, 1))), sem(t, ch, 6), g.up)
            reduce_start(t, g, ch, 5)

    def step6(ch):
        for t, g in reversed(kinds):
            landed(rotated(t, rows(ch, at(g, 2), 0)), sem(t, ch, 7), g.dn)
            landed(rotated(t, rows(ch, at(g, 2), 1)), sem(t, ch, 8), g.up)
            if t == 1:
                sib_rot(ch).start()

    def make_panels(ch):
        v = rot_g.at[chunk_rows(ch), lanes(1 - k)]
        landed(v, sem(1, ch, 9), sib)
        for i in range(SIZES[ch]):
            ds = pl.ds((STARTS[ch] + i) * QUERY_LEN, QUERY_LEN)
            outer = lax.dot_general(
                rot_g[ds], rot_a[ds], (((0,), (0,)), ((), ())), preferred_element_type=F32
            )
            panels[ch % 2, :, pl.ds(i * TILE_J, TILE_J)] = (outer * rcp[...]).astype(BF16)

    def score(ch, h):
        mapped = jnp.dot(
            tg[pl.ds(4 * h, 4)].reshape(4 * BLOCK, TILE_I), panels[ch % 2, :, : SIZES[ch] * TILE_J], preferred_element_type=F32
        )
        acts = ta[pl.ds(4 * h, 4)].reshape(4 * BLOCK, TILE_J).astype(F32)
        for i in range(SIZES[ch]):
            q = STARTS[ch] + i
            total = None
            for j in range(TILE_J // 128):
                term = mapped[:, i * TILE_J + j * 128 : i * TILE_J + (j + 1) * 128] * acts[:, j * 128 : (j + 1) * 128]
                total = term if total is None else total + term
            acc[h, :, q : q + 1] = jnp.sum(total, axis=1, keepdims=True)

    acc[...] = jnp.zeros_like(acc)
    split[...] = jnp.zeros_like(split)

    def train_pair():
        for g in trains:
            g.wait("pair")
            g.start("near1")
        g_tg.sib_start(1)

    def train_near1():
        for g in trains:
            g.wait("near1")
            g.start("far1")
        g_tg.sib_start(4, 5)

    def train_far():
        for g in trains:
            g.wait("far0")
            g.wait("far1")
        g_tg.sib_start(6, 7)

    def train_end():
        g_tg.sib_wait()

    events = {
        "q0": query_pair, "q1": query_own, "t0": train_own, "qf0": query_near0, "qn1": query_pair_in,
        "tp": train_pair_out, "tf0": train_near0, "qf1": query_near1, "qe": query_far, "qw": query_end,
        "tn1": train_pair, "tf1": train_near1, "te": train_far, "tw": train_end,
    }
    steps = {
        "P": partials, "2": step2, "3": step3, "4": step4, "5": step5, "6": step6,
        "N": make_panels, "S": lambda ch: score(ch, 0), "T": lambda ch: score(ch, 1),
    }
    for name in ORDER:
        if name in events:
            events[name]()
        else:
            steps[name[0]](int(name[1:]))

    for h in range(2):
        turned = acc[h].T[:QUERIES]
        for j in range(4):
            blocks[4 * h + j] = turned[:, j * BLOCK : (j + 1) * BLOCK]

    row_moves = ((1, 2), (1, 1), (1, 3), (0, 2), (1, 0), (0, 1), (0, 3))

    def row_peer(a, d):
        return (xl + a) % 2 * 4 + (y + d) % 4

    def to_row(i):
        peer = row_peer(*row_moves[i])
        return remote(blocks.at[peer], first.at[i], FIRST + i, (peer, c))

    for i in range(ROWS - 1):
        to_row(i).start()

    for g in queries + trains:
        g.wait_send()
    for g in (g_qa, g_qg, g_tg):
        g.sib_wait_send()
    basis_copy.wait_send()

    for ch in range(CHUNKS):
        for t, g in kinds:
            for step in range(1, 6):
                for a in reduce_copies(t, g, ch, step):
                    remote(*a).wait_send()
        sib_rot(ch).wait_send()

    total = blocks[r]
    for i in reversed(range(ROWS - 1)):
        a, d = row_moves[i]
        landed(first.at[i], FIRST + i, (row_peer(a, 4 - d), c))
        total = total + first[i]
    total = total / D
    for j in range(COLS):
        split[j, :, :OWNED] = total[:, j * OWNED : (j + 1) * OWNED]

    col_moves = tuple((a, d, e) for a, d in ((1, 2),) + row_moves[1:] + ((0, 0),) for e in (1, 0) if (a, d, e) != (0, 0, 0))

    def col_peer(a, d, e):
        return (xh + a) % 2 * 8 + (z + d) % 4 * 2 + (k + e) % 2

    def to_col(i):
        peer = col_peer(*col_moves[i])
        return remote(split.at[peer], second.at[i], SECOND + i, (r, peer))

    for i in range(COLS - 1):
        to_col(i).start()
    for i in range(ROWS - 1):
        to_row(i).wait_send()
    total = split[c]
    for i in reversed(range(COLS - 1)):
        a, d, e = col_moves[i]
        landed(second.at[i], SECOND + i, (r, col_peer(a, 4 - d, e)))
        total = total + second[i]
    out_ref[...] = total[:, :OWNED]

    for i in range(COLS - 1):
        to_col(i).wait_send()


def shards(*args):
    any_spec = pl.BlockSpec(memory_space=pl.ANY)
    vmem = pltpu.VMEM
    return pl.pallas_call(
        kernel,
        out_shape=jax.ShapeDtypeStruct((QUERIES, OWNED), F32),
        in_specs=[any_spec] * 7,
        out_specs=pl.BlockSpec(memory_space=pltpu.VMEM),
        scratch_shapes=[
            vmem((8, QUERY_LEN, TILE_I), BF16),
            vmem((8, QUERY_LEN, 2 * TILE_J), BF16),
            vmem((TILE_I, TILE_J), BF16),
            vmem((2 * TILE_J, TILE_J), BF16),
            vmem((TILE_I, TILE_J), F32),
            vmem((8, BLOCK, TILE_J), BF16),
            vmem((8, BLOCK, TILE_I), BF16),
            vmem((2, TOKENS, TILE_J), BF16),
            vmem((TOKENS, TILE_J), BF16),
            vmem((TOKENS, TILE_I), BF16),
            vmem((2, 2, TOKENS // 8, TILE_J), BF16),
            vmem((2, 2, TOKENS // 4, TILE_J), BF16),
            vmem((2, TOKENS // 4, TILE_J), BF16),
            vmem((2, TOKENS // 4, TILE_J), BF16),
            vmem((2, TILE_I, max(SIZES) * TILE_J), BF16),
            vmem((2, 4 * BLOCK, 128), F32),
            vmem((ROWS, QUERIES, BLOCK), F32),
            vmem((ROWS - 1, QUERIES, BLOCK), F32),
            vmem((COLS, QUERIES, 128), F32),
            vmem((COLS - 1, QUERIES, 128), F32),
            pltpu.SemaphoreType.DMA((7,)),
            pltpu.SemaphoreType.DMA((N_SEMS,)),
            pltpu.SemaphoreType.DMA((N_SEMS,)),
        ],
        compiler_params=pltpu.CompilerParams(
            collective_id=0, has_side_effects=True, vmem_limit_bytes=62 * 1024 * 1024
        ),
        name="influence",
    )(*args)


def solution(mesh):
    return jax.shard_map(
        shards,
        mesh=mesh,
        in_specs=(
            P("col", "row"),
            P("row", "col"),
            P("row", "col"),
            P("col", "row"),
            P("row", "col"),
            P("row", "col"),
            P("col", "row"),
        ),
        out_specs=P(None, ("row", "col")),
        check_vma=False,
    )
```

```python
import jax
import jax.numpy as jnp
from jax import lax
from jax.experimental import pallas as pl
from jax.experimental.pallas import tpu as pltpu
from jax.sharding import PartitionSpec as P

D = 6144
QUERY_LEN = 256
QUERIES = 8
DAMPING = 0.01

ROWS = 8
COLS = 16
TILE_I = D // ROWS
TILE_J = D // COLS
TOKENS = QUERIES * QUERY_LEN
TRAIN = 2560
BLOCK = TRAIN // 8
OWNED = TRAIN // (ROWS * COLS)

SIZES = (2, 2, 2, 2)
CHUNKS = len(SIZES)
STARTS = tuple(sum(SIZES[:ch]) for ch in range(CHUNKS))

ORDER = (
    "q0", "q1", "t0", "qf0", "tp", "qn1", "tf0", "qf1", "tn1", "qe", "tx", "qw", "P0", "P1",
    "P2", "20", "P3", "21", "22", "30", "23", "31", "32", "40", "33", "50", "41", "tf1",
    "te", "42", "60", "51", "N0", "43", "tw", "S0", "52", "61", "T0", "N1", "53", "S1",
    "62", "T1", "63", "N2", "S2", "T2", "N3", "S3", "T3",
)

MESH = pl.DeviceIdType.MESH
BF16 = jnp.bfloat16
F32 = jnp.float32

AG_A, AG_G, AG_TA, AG_TG = 0, 9, 18, 27
SIB_A, SIB_G, SIB_TG = 36, 44, 52
SIB_BASIS = 60
REDUCE = 61
PER_REDUCE = 10
FIRST = REDUCE + 2 * CHUNKS * PER_REDUCE
SECOND = FIRST + ROWS - 1
N_SEMS = SECOND + COLS - 1


def kernel(
    qa_ref, qg_ref, ab_ref, gb_ref, eig_ref, ta_ref, tg_ref, out_ref,
    qa, qg, ab, gb, rcp, ta, tg, part, rot_a, rot_g, near, mid, mine, other,
    panels, acc, blocks, first, split, second, local, sent, got,
):
    r = lax.axis_index("row")
    c = lax.axis_index("col")
    xl, y = r // 4, r % 4
    xh, z, k = c // 8, (c // 2) % 4, c % 2
    sib = (r, c + 1 - 2 * k)

    class Group:
        pass

    row_g, col_g = Group(), Group()
    row_g.p, row_g.u = xl, y
    row_g.up, row_g.dn = (xl * 4 + (y + 1) % 4, c), (xl * 4 + (y + 3) % 4, c)
    row_g.pair = ((1 - xl) * 4 + y, c)
    col_g.p, col_g.u = xh, z
    col_g.up = (r, xh * 8 + ((z + 1) % 4) * 2 + k)
    col_g.dn = (r, xh * 8 + ((z + 3) % 4) * 2 + k)
    col_g.pair = (r, (1 - xh) * 8 + z * 2 + k)

    def remote(src, dst, i, dev):
        return pltpu.make_async_remote_copy(
            src_ref=src, dst_ref=dst, send_sem=sent.at[i], recv_sem=got.at[i],
            device_id=dev, device_id_type=MESH,
        )

    def lanes(core):
        return pl.ds(pl.multiple_of(core * TILE_J, TILE_J), TILE_J)

    def rows_of(ref, core, size):
        def view(slot, lo, n):
            return ref.at[slot, pl.ds(pl.multiple_of(core * size + lo, 16), n)]

        return view

    def lanes_of(ref, core):
        def view(slot, lo, n):
            return ref.at[slot, pl.ds(lo, n), lanes(core)]

        return view

    def whole(ref):
        def view(slot, lo, n):
            return ref.at[slot, pl.ds(lo, n)]

        return view

    class Gather:
        def __init__(self, g, src, view, view_sib, n, base, sib_base, last="far1"):
            self.last = last
            self.g, self.src, self.view, self.view_sib = g, src, view, view_sib
            self.n, self.base, self.sib_base = n, base, sib_base
            p, u = g.p, g.u
            self.own, self.q1 = p * 4 + u, (1 - p) * 4 + u
            m, o, w = (u + 3) % 4, (u + 1) % 4, (u + 2) % 4
            self.low = (p * 4 + m, (1 - p) * 4 + m)
            self.high = (p * 4 + o, (1 - p) * 4 + o)
            self.far = (p * 4 + w, (1 - p) * 4 + w)

        def full(self, slot):
            return self.view(slot, 0, self.n)

        def half(self, slot, h):
            return self.view(slot, h * (self.n // 2), self.n // 2)

        def copies(self, stage):
            g, b = self.g, self.base
            if stage == "pair":
                return [(self.src, self.full(self.own), b, g.pair)]
            if stage == "near0":
                return [
                    (self.src, self.full(self.own), b + 1, g.up),
                    (self.src, self.full(self.own), b + 2, g.dn),
                ]
            if stage == "near1":
                v = self.full(self.q1)
                return [(v, v, b + 3, g.up), (v, v, b + 4, g.dn)]
            if stage == "cross":
                v = self.full(self.far[0])
                return [(v, v, b + 7, g.pair)]
            i = 0 if stage == "far0" else 1
            lo, hi = self.half(self.low[i], 0), self.half(self.high[i], 1)
            return [(lo, lo, b + 5 + 2 * i, g.up), (hi, hi, b + 6 + 2 * i, g.dn)]

        def start(self, stage):
            for a in self.copies(stage):
                remote(*a).start()

        def wait_send(self):
            for stage in ("pair", "near0", "near1", "far0", self.last):
                for a in self.copies(stage):
                    remote(*a).wait_send()

        def wait(self, stage):
            b, g = self.base, self.g
            if stage == "pair":
                got_ = [(self.full(self.q1), b, g.pair)]
            elif stage == "cross":
                got_ = [(self.full(self.far[1]), b + 7, g.pair)]
            elif stage in ("near0", "near1"):
                i = 0 if stage == "near0" else 1
                got_ = [
                    (self.full(self.low[i]), b + 1 + 2 * i, g.dn),
                    (self.full(self.high[i]), b + 2 + 2 * i, g.up),
                ]
            else:
                i = 0 if stage == "far0" else 1
                got_ = [
                    (self.half(self.far[i], 0), b + 5 + 2 * i, g.dn),
                    (self.half(self.far[i], 1), b + 6 + 2 * i, g.up),
                ]
            for v, i, dev in got_:
                remote(v, v, i, dev).wait_recv()

        def slots(self):
            return (
                self.own, self.q1, self.low[0], self.high[0],
                self.low[1], self.high[1], self.far[0], self.far[1],
            )

        def sib_copy(self, j):
            slot = self.slots()[j]
            src = self.src if j == 0 else self.full(slot)
            return remote(src, self.full(slot), self.sib_base + j, sib)

        def sib_start(self, *js):
            for j in js:
                self.sib_copy(j).start()

        def sib_wait(self):
            for j, slot in enumerate(self.slots()):
                v = self.view_sib(slot, 0, self.n)
                remote(v, v, self.sib_base + j, sib).wait_recv()

        def sib_wait_send(self):
            for j in range(8):
                self.sib_copy(j).wait_send()

    half_q, half_t = QUERY_LEN // 2, BLOCK // 2
    g_qa = Gather(col_g, qa_ref, rows_of(qa, k, half_q), rows_of(qa, 1 - k, half_q), half_q, AG_A, SIB_A)
    g_qg = Gather(row_g, qg_ref, lanes_of(qg, k), lanes_of(qg, 1 - k), QUERY_LEN, AG_G, SIB_G)
    g_ta = Gather(row_g, ta_ref, whole(ta), None, BLOCK, AG_TA, None, "cross")
    g_tg = Gather(col_g, tg_ref, rows_of(tg, k, half_t), rows_of(tg, 1 - k, half_t), half_t, AG_TG, SIB_TG, "cross")
    queries, trains = (g_qa, g_qg), (g_ta, g_tg)

    copies = [
        pltpu.make_async_copy(eig_ref, rcp, local.at[0]),
        pltpu.make_async_copy(qa_ref, g_qa.full(g_qa.own), local.at[1]),
        pltpu.make_async_copy(qg_ref, g_qg.full(g_qg.own), local.at[2]),
        pltpu.make_async_copy(ab_ref, ab, local.at[3]),
        pltpu.make_async_copy(
            gb_ref.at[:, lanes(k)], gb.at[pl.ds(pl.multiple_of(k * TILE_J, TILE_J), TILE_J)], local.at[4]
        ),
        pltpu.make_async_copy(ta_ref, g_ta.full(g_ta.own), local.at[5]),
        pltpu.make_async_copy(tg_ref, g_tg.full(g_tg.own), local.at[6]),
    ]

    barrier = pltpu.get_barrier_semaphore()
    row_peers = [((r + d) % ROWS, c) for d in range(1, ROWS)]
    col_peers = [(r, (c + d) % COLS) for d in range(1, COLS)]
    for dev in row_peers + col_peers:
        pl.semaphore_signal(barrier, inc=1, device_id=dev, device_id_type=MESH)
    for cp in copies:
        cp.start()
    acc[...] = jnp.zeros_like(acc)
    split[...] = jnp.zeros_like(split)
    pl.semaphore_wait(barrier, ROWS + COLS - 2)

    own_basis = gb.at[pl.ds(pl.multiple_of(k * TILE_J, TILE_J), TILE_J)]
    sib_basis = gb.at[pl.ds(pl.multiple_of((1 - k) * TILE_J, TILE_J), TILE_J)]
    basis_copy = remote(gb_ref.at[:, lanes(1 - k)], own_basis, SIB_BASIS, sib)

    def query_pair():
        for g in queries:
            g.start("pair")

    def query_own():
        for g in queries:
            g.start("near0")
            g.sib_start(0)
        basis_copy.start()

    def train_own():
        for g in trains:
            g.start("near0")
        g_tg.sib_start(0)
        copies[0].wait()
        rcp[...] = 1.0 / (QUERY_LEN * (rcp[...] + DAMPING))

    def query_near0():
        for g in queries:
            g.wait("near0")
            g.start("far0")
            g.sib_start(2, 3)

    def query_pair_in():
        for g in queries:
            g.wait("pair")
            g.start("near1")
            g.sib_start(1)

    def train_pair_out():
        for g in trains:
            g.start("pair")

    def train_near0():
        for g in trains:
            g.wait("near0")
            g.start("far0")
        g_tg.sib_start(2, 3)

    def query_near1():
        for g in queries:
            g.wait("near1")
            g.start("far1")
            g.sib_start(4, 5)

    def query_far():
        for g in queries:
            g.wait("far0")
            g.wait("far1")
            g.sib_start(6, 7)

    def query_end():
        for g in queries:
            g.sib_wait()
        remote(sib_basis, sib_basis, SIB_BASIS, sib).wait_recv()
        for cp in copies[1:]:
            cp.wait()

    kinds = ((0, row_g), (1, col_g))

    def sem(t, ch, j):
        return REDUCE + (ch * 2 + t) * PER_REDUCE + j

    def piece(ch):
        return SIZES[ch] * QUERY_LEN // 4

    def rows(ch, v, h=None):
        n = piece(ch)
        lo = STARTS[ch] * QUERY_LEN + v * n
        if h is not None:
            n = n // 2
            lo = lo + h * n
        return pl.ds(pl.multiple_of(lo, 16), n)

    def quarter(ch):
        return pl.ds(STARTS[ch] * QUERY_LEN // 4, piece(ch))

    def eighth(ch):
        return pl.ds(STARTS[ch] * QUERY_LEN // 8, piece(ch) // 2)

    def rotated(t, ds):
        if t == 0:
            return rot_a.at[ds]
        return rot_g.at[ds, lanes(k)]

    def at(g, d):
        return (g.u + d) % 4

    def reduce_copies(t, g, ch, step):
        if step == 1:
            v = at(g, 2)
            return [
                (part.at[t, rows(ch, v, 0)], near.at[t, 0, eighth(ch)], sem(t, ch, 0), g.up),
                (part.at[t, rows(ch, v, 1)], near.at[t, 1, eighth(ch)], sem(t, ch, 1), g.dn),
            ]
        if step == 2:
            return [
                (part.at[t, rows(ch, at(g, 1))], mid.at[t, 0, quarter(ch)], sem(t, ch, 2), g.up),
                (part.at[t, rows(ch, at(g, 3))], mid.at[t, 1, quarter(ch)], sem(t, ch, 3), g.dn),
            ]
        if step == 3:
            return [(mine.at[t, quarter(ch)], other.at[t, quarter(ch)], sem(t, ch, 4), g.pair)]
        if step == 4:
            v = rotated(t, rows(ch, g.u))
            return [(v, v, sem(t, ch, 5), g.up), (v, v, sem(t, ch, 6), g.dn)]
        lo = rotated(t, rows(ch, at(g, 3), 0))
        hi = rotated(t, rows(ch, at(g, 1), 1))
        return [(lo, lo, sem(t, ch, 7), g.up), (hi, hi, sem(t, ch, 8), g.dn)]

    def reduce_start(t, g, ch, step):
        for a in reduce_copies(t, g, ch, step):
            remote(*a).start()

    def landed(v, i, dev):
        remote(v, v, i, dev).wait_recv()

    def chunk_rows(ch):
        return pl.ds(STARTS[ch] * QUERY_LEN, SIZES[ch] * QUERY_LEN)

    def sib_rot(ch):
        v = rot_g.at[chunk_rows(ch), lanes(k)]
        return remote(v, v, sem(1, ch, 9), sib)

    def partials(ch):
        ds = chunk_rows(ch)
        of = pl.ds(STARTS[ch], SIZES[ch])
        for (t, g), ref, basis in zip(kinds, (qa, qg), (ab, gb)):
            part[t, ds] = jnp.dot(
                ref[of].reshape(SIZES[ch] * QUERY_LEN, TILE_I), basis[...], preferred_element_type=F32
            ).astype(BF16)
            reduce_start(t, g, ch, 1)

    def step2(ch):
        for t, g in kinds:
            landed(near.at[t, 0, eighth(ch)], sem(t, ch, 0), g.dn)
            ds = rows(ch, at(g, 1), 0)
            part[t, ds] = (part[t, ds].astype(F32) + near[t, 0, eighth(ch)].astype(F32)).astype(BF16)
            landed(near.at[t, 1, eighth(ch)], sem(t, ch, 1), g.up)
            ds = rows(ch, at(g, 3), 1)
            part[t, ds] = (part[t, ds].astype(F32) + near[t, 1, eighth(ch)].astype(F32)).astype(BF16)
            reduce_start(t, g, ch, 2)

    def step3(ch):
        for t, g in kinds:
            landed(mid.at[t, 0, quarter(ch)], sem(t, ch, 2), g.dn)
            landed(mid.at[t, 1, quarter(ch)], sem(t, ch, 3), g.up)
            total = part[t, rows(ch, g.u)].astype(F32) + mid[t, 0, quarter(ch)].astype(F32) + mid[t, 1, quarter(ch)].astype(F32)
            mine[t, quarter(ch)] = total.astype(BF16)
            reduce_start(t, g, ch, 3)

    def step4(ch):
        for t, g in kinds:
            landed(other.at[t, quarter(ch)], sem(t, ch, 4), g.pair)
            total = (mine[t, quarter(ch)].astype(F32) + other[t, quarter(ch)].astype(F32)).astype(BF16)
            if t == 0:
                rot_a[rows(ch, g.u)] = total
            else:
                rot_g[rows(ch, g.u), lanes(k)] = total
            reduce_start(t, g, ch, 4)

    def step5(ch):
        for t, g in kinds:
            landed(rotated(t, rows(ch, at(g, 3))), sem(t, ch, 5), g.dn)
            landed(rotated(t, rows(ch, at(g, 1))), sem(t, ch, 6), g.up)
            reduce_start(t, g, ch, 5)

    def step6(ch):
        for t, g in reversed(kinds):
            landed(rotated(t, rows(ch, at(g, 2), 0)), sem(t, ch, 7), g.dn)
            landed(rotated(t, rows(ch, at(g, 2), 1)), sem(t, ch, 8), g.up)
            if t == 1:
                sib_rot(ch).start()

    def make_panels(ch):
        v = rot_g.at[chunk_rows(ch), lanes(1 - k)]
        landed(v, sem(1, ch, 9), sib)
        for i in range(SIZES[ch]):
            ds = pl.ds((STARTS[ch] + i) * QUERY_LEN, QUERY_LEN)
            outer = lax.dot_general(
                rot_g[ds], rot_a[ds], (((0,), (0,)), ((), ())), preferred_element_type=F32
            )
            panels[ch % 2, :, pl.ds(i * TILE_J, TILE_J)] = (outer * rcp[...]).astype(BF16)

    def score(ch, h):
        mapped = jnp.dot(
            tg[pl.ds(4 * h, 4)].reshape(4 * BLOCK, TILE_I), panels[ch % 2, :, : SIZES[ch] * TILE_J], preferred_element_type=F32
        )
        acts = ta[pl.ds(4 * h, 4)].reshape(4 * BLOCK, TILE_J).astype(F32)
        for i in range(SIZES[ch]):
            q = STARTS[ch] + i
            total = None
            for j in range(TILE_J // 128):
                term = mapped[:, i * TILE_J + j * 128 : i * TILE_J + (j + 1) * 128] * acts[:, j * 128 : (j + 1) * 128]
                total = term if total is None else total + term
            acc[h, :, q : q + 1] = jnp.sum(total, axis=1, keepdims=True)


    def train_pair():
        for g in trains:
            g.wait("pair")
            g.start("near1")
        g_tg.sib_start(1)

    def train_near1():
        for g in trains:
            g.wait("near1")
        g_tg.sib_start(4, 5)

    def train_cross():
        for g in trains:
            g.wait("far0")
            g.start("cross")
        g_tg.sib_start(6)

    def train_far():
        for g in trains:
            g.wait("cross")
        g_tg.sib_start(7)

    def train_end():
        g_tg.sib_wait()

    events = {
        "q0": query_pair, "q1": query_own, "t0": train_own, "qf0": query_near0, "qn1": query_pair_in,
        "tp": train_pair_out, "tf0": train_near0, "qf1": query_near1, "qe": query_far, "qw": query_end,
        "tn1": train_pair, "tf1": train_near1, "te": train_far, "tx": train_cross, "tw": train_end,
    }
    steps = {
        "P": partials, "2": step2, "3": step3, "4": step4, "5": step5, "6": step6,
        "N": make_panels, "S": lambda ch: score(ch, 0), "T": lambda ch: score(ch, 1),
    }
    for name in ORDER:
        if name in events:
            events[name]()
        else:
            steps[name[0]](int(name[1:]))

    for h in range(2):
        turned = acc[h].T[:QUERIES]
        for j in range(4):
            blocks[4 * h + j] = turned[:, j * BLOCK : (j + 1) * BLOCK]

    row_moves = ((1, 2), (1, 1), (1, 3), (0, 2), (1, 0), (0, 1), (0, 3))

    def row_peer(a, d):
        return (xl + a) % 2 * 4 + (y + d) % 4

    def to_row(i):
        peer = row_peer(*row_moves[i])
        return remote(blocks.at[peer], first.at[i], FIRST + i, (peer, c))

    for i in range(ROWS - 1):
        to_row(i).start()

    for g in queries + trains:
        g.wait_send()
    for g in (g_qa, g_qg, g_tg):
        g.sib_wait_send()
    basis_copy.wait_send()

    for ch in range(CHUNKS):
        for t, g in kinds:
            for step in range(1, 6):
                for a in reduce_copies(t, g, ch, step):
                    remote(*a).wait_send()
        sib_rot(ch).wait_send()

    total = blocks[r]
    for i in reversed(range(ROWS - 1)):
        a, d = row_moves[i]
        landed(first.at[i], FIRST + i, (row_peer(a, 4 - d), c))
        total = total + first[i]
    total = total / D
    for j in range(COLS):
        split[j, :, :OWNED] = total[:, j * OWNED : (j + 1) * OWNED]

    col_moves = tuple((a, d, e) for a, d in ((1, 2),) + row_moves[1:] + ((0, 0),) for e in (1, 0) if (a, d, e) != (0, 0, 0))

    def col_peer(a, d, e):
        return (xh + a) % 2 * 8 + (z + d) % 4 * 2 + (k + e) % 2

    def to_col(i):
        peer = col_peer(*col_moves[i])
        return remote(split.at[peer], second.at[i], SECOND + i, (r, peer))

    for i in range(COLS - 1):
        to_col(i).start()
    for i in range(ROWS - 1):
        to_row(i).wait_send()
    total = split[c]
    for i in reversed(range(COLS - 1)):
        a, d, e = col_moves[i]
        landed(second.at[i], SECOND + i, (r, col_peer(a, 4 - d, e)))
        total = total + second[i]
    out_ref[...] = total[:, :OWNED]

    for i in range(COLS - 1):
        to_col(i).wait_send()


def shards(*args):
    any_spec = pl.BlockSpec(memory_space=pl.ANY)
    vmem = pltpu.VMEM
    return pl.pallas_call(
        kernel,
        out_shape=jax.ShapeDtypeStruct((QUERIES, OWNED), F32),
        in_specs=[any_spec] * 7,
        out_specs=pl.BlockSpec(memory_space=pltpu.VMEM),
        scratch_shapes=[
            vmem((8, QUERY_LEN, TILE_I), BF16),
            vmem((8, QUERY_LEN, 2 * TILE_J), BF16),
            vmem((TILE_I, TILE_J), BF16),
            vmem((2 * TILE_J, TILE_J), BF16),
            vmem((TILE_I, TILE_J), F32),
            vmem((8, BLOCK, TILE_J), BF16),
            vmem((8, BLOCK, TILE_I), BF16),
            vmem((2, TOKENS, TILE_J), BF16),
            vmem((TOKENS, TILE_J), BF16),
            vmem((TOKENS, TILE_I), BF16),
            vmem((2, 2, TOKENS // 8, TILE_J), BF16),
            vmem((2, 2, TOKENS // 4, TILE_J), BF16),
            vmem((2, TOKENS // 4, TILE_J), BF16),
            vmem((2, TOKENS // 4, TILE_J), BF16),
            vmem((2, TILE_I, max(SIZES) * TILE_J), BF16),
            vmem((2, 4 * BLOCK, 128), F32),
            vmem((ROWS, QUERIES, BLOCK), F32),
            vmem((ROWS - 1, QUERIES, BLOCK), F32),
            vmem((COLS, QUERIES, 128), F32),
            vmem((COLS - 1, QUERIES, 128), F32),
            pltpu.SemaphoreType.DMA((7,)),
            pltpu.SemaphoreType.DMA((N_SEMS,)),
            pltpu.SemaphoreType.DMA((N_SEMS,)),
        ],
        compiler_params=pltpu.CompilerParams(
            collective_id=0, has_side_effects=True, vmem_limit_bytes=62 * 1024 * 1024
        ),
        name="influence",
    )(*args)


def solution(mesh):
    return jax.shard_map(
        shards,
        mesh=mesh,
        in_specs=(
            P("col", "row"),
            P("row", "col"),
            P("row", "col"),
            P("col", "row"),
            P("row", "col"),
            P("row", "col"),
            P("col", "row"),
        ),
        out_specs=P(None, ("row", "col")),
        check_vma=False,
    )
```
